32 devices in a mesh: patch: 8 (over z, y), coarse: 4 (over x, core).
Axes of the slice: x: 2, y: 2, z: 4, core: 2. Of those that a mesh axis runs over, the one named last changes fastest.
Arguments:
- residual: bfloat16 [2, 2, 49152, 256], P(None, None, ('patch', 'coarse')), may hold values from -6 to 6
- patch_inv: bfloat16 [128, 2, 1024, 1024], P(('patch', 'coarse')), may hold values from -0.1875 to 0.1875
- coarse_basis: bfloat16 [128, 2, 1024, 32], P(('patch', 'coarse')), may hold values from -0.1875 to 0.1875
- coarse_inv: bfloat16 [64, 2, 32, 32], P('coarse'), may hold values from -1 to 1
- patch_slots: int32 [128, 512], P(('patch', 'coarse')), may hold values from 0 to 1791, as said below
- send_rows: int32 [32, 2, 128], P(('patch', 'coarse')), may hold values from 0 to 1535, as said below
- coarse_block: int32 [128], P(('patch', 'coarse')), may hold values from 0 to 63
Outputs:
- correction: bfloat16 [2, 2, 49152, 256], P(None, None, ('patch', 'coarse'))
The draws below stay inside these ranges and needn't reach their ends.
Inputs may be any that keep to these rules, and one draw needn't show every extreme that they name: `send_rows`: within each of the two blocks of a device the 128 rows are distinct. `patch_slots`: the 512 positions of a patch are distinct; they hold its device's rows (p mod 4) * 384 to (p mod 4 + 1) * 384 - 1, 64 positions of 1536 or more, and other rows of its device below 1536; each position of 1536 or more is used by exactly one patch of the device.
All inputs are finite; a program needn't handle non-finite values.
Results may differ from the reference program's by a relative error of at most 0.006.
Values may be sent and summed in bfloat16 or wider, within the bound.
No kernel may reach another device: no remote copies, remote signals or barrier semaphores. Data moves between devices by JAX's collectives and lax.ppermute only.
A program may use at most 128 MiB of HBM per device.

```python
import jax
import jax.numpy as jnp
from jax import lax

PN = 512
CORE = 384
SLOT = 128
WAVES = 2
CD = 16
PATCH_DEV = 4
RHS = 256
NODE_DEV = 1536
EXT = 1792
REMOTE = 64
PATCHES = 128
NODES = 49152
NBLK = 64


def distinct_order(key, shape):
    length = shape[-1]
    scores = jax.random.randint(key, shape, 0, 1 << 19) * length + jnp.arange(length, dtype=jnp.int32)
    return jnp.argsort(scores, axis=-1, stable=True).astype(jnp.int32)


def draw_send_rows(key, part):
    device_count = PATCHES // PATCH_DEV
    ordering = distinct_order(jax.random.fold_in(key, 5), (device_count, 2, NODE_DEV))
    return ordering[:, :, :SLOT].astype(jnp.int32)


def draw_patch_slots(key, part):
    device_count = PATCHES // PATCH_DEV
    far_count = 2 * SLOT
    far_order = distinct_order(jax.random.fold_in(key, 11), (device_count, far_count))
    remote = NODE_DEV + far_order.reshape(device_count, PATCH_DEV, REMOTE)
    own_count = PN - CORE - REMOTE
    others = NODE_DEV - CORE
    chosen = distinct_order(jax.random.fold_in(key, 13), (device_count, PATCH_DEV, others))[:, :, :own_count]
    patch_index = jnp.arange(PATCH_DEV, dtype=jnp.int32)[None, :, None]
    chosen = jnp.where(chosen >= patch_index * CORE, chosen + CORE, chosen)
    core_rows = jnp.broadcast_to(patch_index * CORE + jnp.arange(CORE, dtype=jnp.int32)[None, None, :], (device_count, PATCH_DEV, CORE))
    listing = jnp.concatenate([core_rows, remote, chosen], axis=-1)
    ordering = distinct_order(jax.random.fold_in(key, 17), (device_count, PATCH_DEV, PN))
    listing = jnp.take_along_axis(listing, ordering, axis=-1)
    return listing.reshape(PATCHES, PN).astype(jnp.int32)


def touch_ends(entries, key, low, largest):
    shape = entries.shape
    index_at = [jax.random.randint(jax.random.fold_in(key, axis), (), 0, shape[axis]) for axis in range(len(shape))]
    entries = entries.at[tuple(index_at)].set(low)
    longest = shape.index(max(shape))
    index_at[longest] = (index_at[longest] + 1) % shape[longest]
    return entries.at[tuple(index_at)].set(largest)


def shard_levels(stream_key, shape, cuts, low, high):
    level = 1.0
    for axis_at, shards_of in cuts:
        steps = jax.random.uniform(jax.random.fold_in(jax.random.fold_in(stream_key, 6), axis_at), (shards_of,), jnp.float32, low / len(cuts), high / len(cuts))
        level = level * jnp.repeat(jnp.exp(steps), shape[axis_at] // shards_of).reshape((-1,) + (1,) * (len(shape) - 1 - axis_at))
    return level


def bell_draw(rng, shape, deviation, bound, split=(), held_as=jnp.bfloat16):
    level = shard_levels(rng, shape, split, -0.22, 0.18) if split else 1.0
    drawn = jax.random.normal(rng, shape, jnp.float32) * deviation * level
    return jnp.minimum(jnp.maximum(drawn, -bound), bound).astype(held_as)


def setup_inputs(seed: int = 0) -> dict:
    keys = jax.random.split(jax.random.key(seed), 8)
    residual = bell_draw(keys[0], (WAVES, 2, NODES, RHS), 1.0, 6.0, ((2, 32),))
    patch_inv = bell_draw(keys[1], (PATCHES, WAVES, 2 * PN, 2 * PN), (2 * PN) ** -0.5, 0.1875, ((0, 32),))
    coarse_basis = bell_draw(keys[2], (PATCHES, WAVES, 2 * PN, 2 * CD), (2 * PN) ** -0.5, 0.1875, ((0, 32),))
    coarse_inv = bell_draw(keys[3], (NBLK, WAVES, 2 * CD, 2 * CD), (2 * CD) ** -0.5, 1.0, ((0, 4),))
    patch_slots = draw_patch_slots(jax.random.fold_in(keys[7], 71), 0)
    send_rows = draw_send_rows(jax.random.fold_in(keys[7], 71), 0)
    coarse_block = touch_ends(jax.random.randint(keys[6], (PATCHES,), 0, NBLK), jax.random.fold_in(keys[6], 1), 0, NBLK - 1).astype(jnp.int32)
    return {"residual": residual, "patch_inv": patch_inv, "coarse_basis": coarse_basis, "coarse_inv": coarse_inv, "patch_slots": patch_slots, "send_rows": send_rows, "coarse_block": coarse_block}


def reference(residual, patch_inv, coarse_basis, coarse_inv, patch_slots, send_rows, coarse_block):
    device_count = PATCHES // PATCH_DEV
    node_data = residual.reshape(WAVES, 2, device_count, NODE_DEV, RHS)
    device_ids = jnp.arange(device_count, dtype=jnp.int32)
    highest = lax.Precision.HIGHEST

    def gather_patches(device):
        below = (device - 1) % device_count
        above = (device + 1) % device_count
        own_rows = node_data[:, :, device]
        from_below = jnp.take(node_data[:, :, below], send_rows[below, 0], axis=2)
        from_above = jnp.take(node_data[:, :, above], send_rows[above, 1], axis=2)
        extended = jnp.concatenate([own_rows, from_below, from_above], axis=2)
        slot_list = lax.dynamic_slice_in_dim(patch_slots, device * PATCH_DEV, PATCH_DEV, 0)
        return jnp.take(extended, slot_list, axis=2), slot_list

    def basis_of(device):
        basis_rows = lax.dynamic_slice_in_dim(coarse_basis, device * PATCH_DEV, PATCH_DEV, 0)
        return basis_rows.astype(jnp.float32).reshape(PATCH_DEV, WAVES, 2, PN, 2 * CD)

    def restrict(device):
        gathered, slot_list = gather_patches(device)
        return jnp.einsum('pwqnc,wqpnr->pwcr', basis_of(device), gathered.astype(jnp.float32), precision=highest)

    patch_parts = lax.map(restrict, device_ids).reshape(PATCHES, WAVES, 2 * CD, RHS)
    coarse_sums = jax.ops.segment_sum(patch_parts, coarse_block, NBLK)
    coarse_coef = jnp.einsum('bwcd,bwdr->bwcr', coarse_inv.astype(jnp.float32), coarse_sums, precision=highest).astype(jnp.bfloat16)

    def correct(device):
        gathered, slot_list = gather_patches(device)
        inverse = lax.dynamic_slice_in_dim(patch_inv, device * PATCH_DEV, PATCH_DEV, 0)
        inverse = inverse.astype(jnp.float32).reshape(PATCH_DEV, WAVES, 2, PN, 2, PN)
        local_terms = jnp.einsum('pwabqn,wqpnr->wapbr', inverse, gathered.astype(jnp.float32), precision=highest)
        block_ids = lax.dynamic_slice_in_dim(coarse_block, device * PATCH_DEV, PATCH_DEV, 0)
        patch_coef = jnp.take(coarse_coef, block_ids, axis=0).astype(jnp.float32)
        local_terms = local_terms + jnp.einsum('pwqnc,pwcr->wqpnr', basis_of(device), patch_coef, precision=highest)
        collected = jnp.zeros((WAVES, 2, EXT, RHS), jnp.float32).at[:, :, slot_list].add(local_terms)
        return collected[:, :, :NODE_DEV], collected[:, :, NODE_DEV:NODE_DEV + SLOT], collected[:, :, NODE_DEV + SLOT:]

    own_terms, to_lower, to_upper = lax.map(correct, device_ids)

    def finish(device):
        below = (device - 1) % device_count
        above = (device + 1) % device_count
        summed = own_terms[device]
        summed = summed.at[:, :, send_rows[device, 0]].add(to_lower[above])
        summed = summed.at[:, :, send_rows[device, 1]].add(to_upper[below])
        return summed.astype(jnp.bfloat16)

    finished = lax.map(finish, device_ids)
    return jnp.moveaxis(finished, 0, 2).reshape(WAVES, 2, NODES, RHS)
```

```python
import functools

import jax
import jax.numpy as jnp
from jax import lax
from jax.experimental import pallas as pl
from jax.experimental.pallas import tpu as pltpu
from jax.sharding import PartitionSpec as P

AXES = ("patch", "coarse")
LANES = 128
F32 = jnp.float32
BF16 = jnp.bfloat16


def passed_along(value, axis, steps):
    count = lax.axis_size(axis)
    pairs = [(source, (source + steps) % count) for source in range(count)]
    return lax.ppermute(value, axis, pairs)


def dot(a, b):
    return jnp.dot(a, b, preferred_element_type=F32)


def as_column(row):
    return jnp.transpose(jnp.broadcast_to(row, (LANES, row.shape[1])))


def iota(shape, axis):
    return lax.broadcasted_iota(jnp.int32, shape, axis)


def one_hot_rows(column, width, start=0):
    rows = column.shape[0]
    parts = [
        (column == (iota((rows, LANES), 1) + (start + t)).astype(F32)).astype(F32).astype(BF16)
        for t in range(0, width, LANES)
    ]
    return jnp.concatenate(parts, axis=1)


def vmem(shape, dtype):
    return pltpu.VMEM(shape, dtype)


def whole(array):
    zeros = (0,) * array.ndim
    return pl.BlockSpec(array.shape, lambda *_: zeros)


def select_kernel(rows_ref, x_ref, up_ref, down_ref, sel):
    slots = rows_ref.shape[1]
    nodes = x_ref.shape[1]

    @pl.when(pl.program_id(0) == 0)
    def _():
        for b in range(2):
            col = as_column(rows_ref[b : b + 1, :].astype(F32))
            sel[b * slots : (b + 1) * slots, :] = one_hot_rows(col, nodes)

    got = dot(sel[...], x_ref[0]).astype(BF16)
    up_ref[0] = got[:slots]
    down_ref[0] = got[slots:]


def select_rows(x4, rows):
    parts, nodes, width = x4.shape
    slots = rows.shape[1]
    block = pl.BlockSpec((1, slots, width), lambda i: (i, 0, 0))
    shape = jax.ShapeDtypeStruct((parts, slots, width), BF16)
    return pl.pallas_call(
        select_kernel,
        grid=(parts,),
        in_specs=[whole(rows), pl.BlockSpec((1, nodes, width), lambda i: (i, 0, 0))],
        out_specs=[block, block],
        out_shape=[shape, shape],
        scratch_shapes=[vmem((2 * slots, nodes), BF16)],
        name="select",
    )(rows, x4)


def prep_kernel(
    core, slots_ref, basis_ref, x_ref,
    pos_ref, rest_ref, crem_ref, y_ref, r_ref, btrem_ref, bext_ref,
    ccat, bt,
):
    patches, patch_nodes = slots_ref.shape
    waves, width = basis_ref.shape[1], basis_ref.shape[2]
    nodes = x_ref.shape[1]
    rest = patch_nodes - core
    ext = ccat.shape[1]
    step = pl.program_id(0)

    @pl.when(step == 0)
    def _():
        slots = slots_ref[...].astype(F32)
        first = (iota((patches, patch_nodes), 0) * core).astype(F32)
        local = slots - first
        outside = (local < 0.0) | (local >= float(core))
        before = (iota((patch_nodes, patch_nodes), 0) < iota((patch_nodes, patch_nodes), 1))
        rank = dot(
            outside.astype(F32).astype(BF16), before.astype(F32).astype(BF16)
        )
        pos = jnp.where(outside, rank + float(core), local)
        pos_ref[...] = pos
        for p in range(patches):
            prow = pos[p : p + 1, :]
            srow = slots[p : p + 1, :]
            permute = one_hot_rows(as_column(prow), patch_nodes)
            basis = jnp.concatenate(
                [
                    basis_ref[p, w, :, q * patch_nodes : (q + 1) * patch_nodes]
                    for w in range(waves)
                    for q in range(2)
                ],
                axis=0,
            )
            moved = dot(basis, permute).astype(BF16)
            hit = prow == (iota((rest, patch_nodes), 0) + core).astype(F32)
            ids = jnp.sum(
                jnp.where(hit, jnp.broadcast_to(srow, hit.shape), 0.0), axis=1, keepdims=True
            )
            ids = jnp.broadcast_to(ids, (rest, LANES))
            rest_ref[:, p * rest : (p + 1) * rest] = jnp.transpose(ids)[0:8]
            pick = one_hot_rows(ids, ext)
            ccat[p * rest : (p + 1) * rest, :] = pick
            spread = dot(moved[:, core:], pick).astype(BF16)
            for k in range(waves * 2):
                rows = slice(k * width, (k + 1) * width)
                here = slice(p * width, (p + 1) * width)
                bt[k, here, :] = spread[rows]
                bt[k, here, p * core : (p + 1) * core] = (
                    spread[rows, p * core : (p + 1) * core] + moved[rows, :core]
                )
        crem_ref[...] = ccat[:, nodes:]

    x = x_ref[0]
    y_ref[0] = dot(ccat[:, :nodes], x).astype(BF16)
    mine = bt[step]
    part = dot(mine[:, :nodes], x)

    @pl.when(step % 2 == 0)
    def _():
        r_ref[0] = part

    @pl.when(step % 2 == 1)
    def _():
        r_ref[0] = r_ref[0] + part

    btrem_ref[0] = mine[:, nodes:]
    bext_ref[0] = jnp.transpose(mine)


def prepare(slots, basis_t, x4, ext):
    parts, nodes, width = x4.shape
    patches, patch_nodes = slots.shape
    core = nodes // patches
    rest = patch_nodes - core
    columns = patches * basis_t.shape[2]
    rows3 = lambda a, b: pl.BlockSpec((1, a, b), lambda i: (i, 0, 0))
    shape = jax.ShapeDtypeStruct
    return pl.pallas_call(
        functools.partial(prep_kernel, core),
        grid=(parts,),
        in_specs=[whole(slots), whole(basis_t), rows3(nodes, width)],
        out_specs=[
            pl.BlockSpec((patches, patch_nodes), lambda i: (0, 0)),
            pl.BlockSpec((8, patches * rest), lambda i: (0, 0)),
            pl.BlockSpec((patches * rest, ext - nodes), lambda i: (0, 0)),
            rows3(patches * rest, width),
            pl.BlockSpec((1, columns, width), lambda i: (i // 2, 0, 0)),
            rows3(columns, ext - nodes),
            rows3(ext, columns),
        ],
        out_shape=[
            shape((patches, patch_nodes), F32),
            shape((8, patches * rest), F32),
            shape((patches * rest, ext - nodes), BF16),
            shape((parts, patches * rest, width), BF16),
            shape((parts // 2, columns, width), F32),
            shape((parts, columns, ext - nodes), BF16),
            shape((parts, ext, columns), BF16),
        ],
        scratch_shapes=[vmem((patches * rest, ext), BF16), vmem((parts, columns, ext), BF16)],
        name="prep",
    )(slots, basis_t, x4)


def owner_order(columns, patches, width, per_group):
    rows = patches * per_group
    i = iota((columns, columns), 0)
    j = iota((columns, columns), 1)
    source = ((i % rows) // per_group) * width + (i // rows) * per_group + i % per_group
    return (source == j).astype(F32).astype(BF16)


def restrict_kernel(per_group, block_ref, r_ref, btrem_ref, below_ref, above_ref, out_ref):
    waves, columns, width = r_ref.shape
    patches = block_ref.shape[0]
    slots = below_ref.shape[1]
    rows = patches * per_group
    groups = columns // rows
    halves = width // LANES
    order = owner_order(columns, patches, columns // patches, per_group)
    tail = out_ref.shape[1] - rows
    keys = jnp.zeros((tail, LANES), F32)
    for p in range(patches):
        keys = jnp.where(iota((tail, LANES), 0) == p, block_ref[p].astype(F32), keys)
    keys = keys.astype(BF16)
    for w in range(waves):
        total = r_ref[w]
        for q in range(2):
            k = 2 * w + q
            total = total + dot(btrem_ref[k, :, :slots], below_ref[k])
            total = total + dot(btrem_ref[k, :, slots:], above_ref[k])
        moved = dot(order, total.astype(BF16)).astype(BF16)
        for g in range(groups):
            for h in range(halves):
                owner = (w * groups + g) * halves + h
                out_ref[owner, :rows, :] = moved[g * rows : (g + 1) * rows, h * LANES : (h + 1) * LANES]
                out_ref[owner, rows:, :] = keys


def restrict(block, r_own, bt_rem, below, above, owners, per_group, padded):
    return pl.pallas_call(
        functools.partial(restrict_kernel, per_group),
        in_specs=[pl.BlockSpec(memory_space=pltpu.SMEM)] + [pl.BlockSpec(memory_space=pltpu.VMEM)] * 4,
        out_specs=pl.BlockSpec(memory_space=pltpu.VMEM),
        out_shape=jax.ShapeDtypeStruct((owners, padded, LANES), BF16),
        name="restrict",
    )(block, r_own, bt_rem, below, above)


def sums_kernel(per_group, patches, got_ref, out_ref, data, tags):
    owners, padded, _ = got_ref.shape
    rows = patches * per_group
    tail = padded - rows
    for s in range(owners):
        data[s * rows : (s + 1) * rows, :] = got_ref[s, :rows, :].astype(F32)
        tags[s * tail : (s + 1) * tail, :] = got_ref[s, rows:, :].astype(F32)
    count = owners * rows
    i = iota((count, owners * tail), 0)
    j = iota((count, owners * tail), 1)
    wanted = (i // rows) * tail + (i % rows) // per_group
    keys = dot((wanted == j).astype(F32).astype(BF16), tags[...].astype(BF16))
    keys = keys * float(per_group) + (iota((count, LANES), 0) % per_group).astype(F32)
    key_row = jnp.transpose(keys)[0:1, :]
    column = jnp.concatenate([keys] * (count // LANES), axis=1)
    same = (column == key_row).astype(F32).astype(BF16)
    sums = dot(same, data[...].astype(BF16))
    data[...] = sums
    for s in range(owners):
        out_ref[s] = data[s * rows : (s + 1) * rows, :].astype(BF16)


def owner_sums(got, patches, per_group):
    owners, padded, _ = got.shape
    rows = patches * per_group
    return pl.pallas_call(
        functools.partial(sums_kernel, per_group, patches),
        in_specs=[pl.BlockSpec(memory_space=pltpu.VMEM)],
        out_specs=pl.BlockSpec(memory_space=pltpu.VMEM),
        out_shape=jax.ShapeDtypeStruct((owners, rows, LANES), BF16),
        scratch_shapes=[
            vmem((owners * rows, LANES), F32),
            vmem((owners * (padded - rows), LANES), F32),
        ],
        name="sums",
    )(got)


def local_kernel(pos_ref, core_ref, y_ref, crem_ref, below_ref, above_ref, inv_ref, out_ref, pm, g):
    core, width = core_ref.shape[1], core_ref.shape[2]
    patch_nodes = pos_ref.shape[2]
    slots = below_ref.shape[1]
    prow = pos_ref[0]

    @pl.when(pl.program_id(1) == 0)
    def _():
        pm[...] = one_hot_rows(as_column(prow), patch_nodes)

    crem = crem_ref[...]
    for q in range(2):
        far = dot(crem[:, :slots], below_ref[q]) + dot(crem[:, slots:], above_ref[q])
        other = y_ref[q] + far.astype(BF16)
        ordered = jnp.concatenate([core_ref[q], other], axis=0)
        g[q * patch_nodes : (q + 1) * patch_nodes, :] = dot(pm[...], ordered).astype(BF16)
    local = dot(inv_ref[0, 0], g[...]).astype(BF16)
    back = (prow == iota((patch_nodes, patch_nodes), 0).astype(F32)).astype(F32).astype(BF16)
    for q in range(2):
        out_ref[0, q] = dot(back, local[q * patch_nodes : (q + 1) * patch_nodes]).astype(BF16)


def local_products(pos, x4, y, crem, below, above, patch_inv, first, count):
    parts, nodes, width = x4.shape
    patches, waves = patch_inv.shape[:2]
    patch_nodes = pos.shape[1]
    core = nodes // patches
    rest = patch_nodes - core
    slots = below.shape[1]
    pos3 = pos.reshape(patches, 1, patch_nodes)
    return pl.pallas_call(
        local_kernel,
        grid=(count, waves),
        in_specs=[
            pl.BlockSpec((1, 1, patch_nodes), lambda p, w: (first + p, 0, 0)),
            pl.BlockSpec((2, core, width), lambda p, w: (w, first + p, 0)),
            pl.BlockSpec((2, rest, width), lambda p, w: (w, first + p, 0)),
            pl.BlockSpec((rest, 2 * slots), lambda p, w: (first + p, 0)),
            pl.BlockSpec((2, slots, width), lambda p, w: (w, 0, 0)),
            pl.BlockSpec((2, slots, width), lambda p, w: (w, 0, 0)),
            pl.BlockSpec((1, 1) + patch_inv.shape[2:], lambda p, w: (first + p, w, 0, 0)),
        ],
        out_specs=pl.BlockSpec((1, 2, patch_nodes, width), lambda p, w: (p, w, 0, 0)),
        out_shape=jax.ShapeDtypeStruct((count, parts, patch_nodes, width), BF16),
        scratch_shapes=[
            vmem((patch_nodes, patch_nodes), BF16),
            vmem((2 * patch_nodes, width), BF16),
        ],
        name="local",
    )(pos3, x4, y, crem, below, above, patch_inv)


def scatter_kernel(nodes, rest_ref, *refs):
    *local_refs, own_ref, margin_ref, spread = refs
    core = nodes // sum(r.shape[0] for r in local_refs)
    ext, columns = spread.shape

    @pl.when(pl.program_id(0) == 0)
    def _():
        ids = rest_ref[0:1, :]
        spread[...] = (ids == iota((ext, columns), 0).astype(F32)).astype(F32).astype(BF16)

    blocks = [(r, i) for r in local_refs for i in range(r.shape[0])]
    others = jnp.concatenate([r[i, 0, core:, :] for r, i in blocks], axis=0)
    total = dot(spread[...], others)
    for p, (r, i) in enumerate(blocks):
        rows = slice(p * core, (p + 1) * core)
        own_ref[0, rows, :] = (total[rows] + r[i, 0, :core, :].astype(F32)).astype(BF16)
    margin_ref[0] = total[nodes:]


def scatter(rest_ids, locals_, nodes, ext):
    parts, patch_nodes, width = locals_[0].shape[1:]
    columns = rest_ids.shape[1]
    return pl.pallas_call(
        functools.partial(scatter_kernel, nodes),
        grid=(parts,),
        in_specs=[whole(rest_ids)]
        + [pl.BlockSpec((a.shape[0], 1, patch_nodes, width), lambda i: (0, i, 0, 0)) for a in locals_],
        out_specs=[
            pl.BlockSpec((1, nodes, width), lambda i: (i, 0, 0)),
            pl.BlockSpec((1, ext - nodes, width), lambda i: (i, 0, 0)),
        ],
        out_shape=[
            jax.ShapeDtypeStruct((parts, nodes, width), BF16),
            jax.ShapeDtypeStruct((parts, ext - nodes, width), F32),
        ],
        scratch_shapes=[vmem((ext, columns), BF16)],
        name="scatter",
    )(rest_ids, *locals_)


def coef_kernel(
    per_group, block_ref, place_ref, sums_ref, inv_ref, brem_ref, margin_ref,
    coef_ref, low_ref, high_ref, gathered, inverse,
):
    waves, columns, width = coef_ref.shape
    patches = block_ref.shape[0]
    group, each = inv_ref.shape[0], inv_ref.shape[1]
    size = inv_ref.shape[3]
    rows = patches * per_group
    groups = columns // rows
    halves = width // LANES
    slots = low_ref.shape[1]
    order = owner_order(columns, patches, size, per_group)
    inverse[...] = jnp.zeros(inverse.shape, inverse.dtype)
    for w in range(waves):
        for p in range(patches):
            block = block_ref[p]
            piece = lax.rem(block // each - place_ref[0] + group, group)
            inverse[p * size : (p + 1) * size, p * size : (p + 1) * size] = inv_ref[
                piece, lax.rem(block, each), w
            ].astype(F32)
        for g in range(groups):
            for h in range(halves):
                gathered[g * rows : (g + 1) * rows, h * LANES : (h + 1) * LANES] = sums_ref[
                    (w * groups + g) * halves + h
                ].astype(F32)
        mixed = dot(inverse[...].astype(BF16), jnp.transpose(order)).astype(BF16)
        coef = dot(mixed, gathered[...].astype(BF16)).astype(BF16)
        coef_ref[w] = coef
        for q in range(2):
            k = 2 * w + q
            low_ref[k] = (margin_ref[k, :slots, :] + dot(brem_ref[k, :slots, :], coef)).astype(BF16)
            high_ref[k] = (margin_ref[k, slots:, :] + dot(brem_ref[k, slots:, :], coef)).astype(BF16)


def coefficients(block, place, sums, inverses, b_ext, margin, nodes, per_group):
    parts, ext, columns = b_ext.shape
    width = margin.shape[2]
    waves = inverses.shape[2]
    slots = (ext - nodes) // 2
    shape = jax.ShapeDtypeStruct
    full = pl.BlockSpec(memory_space=pltpu.VMEM)
    zero = lambda a: pl.BlockSpec(a, lambda *_: (0,) * len(a))
    return pl.pallas_call(
        functools.partial(coef_kernel, per_group),
        grid=(1,),
        in_specs=[
            pl.BlockSpec(memory_space=pltpu.SMEM),
            pl.BlockSpec(memory_space=pltpu.SMEM),
            zero(sums.shape),
            zero(inverses.shape),
            pl.BlockSpec((parts, ext - nodes, columns), lambda i: (0, nodes // (ext - nodes), 0)),
            zero(margin.shape),
        ],
        out_specs=[
            zero((waves, columns, width)),
            zero((parts, slots, width)),
            zero((parts, slots, width)),
        ],
        out_shape=[
            shape((waves, columns, width), BF16),
            shape((parts, slots, width), BF16),
            shape((parts, slots, width), BF16),
        ],
        scratch_shapes=[vmem((columns, width), F32), vmem((columns, columns), F32)],
        name="coef",
    )(block, place, sums, inverses, b_ext, margin)


def final_kernel(rows_ref, own_ref, b_ref, coef_ref, above_ref, below_ref, out_ref, spread):
    slots = rows_ref.shape[1]
    nodes = own_ref.shape[1]

    @pl.when(pl.program_id(0) == 0)
    def _():
        for b in range(2):
            ids = rows_ref[b : b + 1, :].astype(F32)
            spread[:, b * slots : (b + 1) * slots] = (
                (ids == iota((nodes, slots), 0).astype(F32)).astype(F32).astype(BF16)
            )

    back = jnp.concatenate([above_ref[0], below_ref[0]], axis=0)
    total = own_ref[0].astype(F32) + dot(spread[...], back) + dot(b_ref[0], coef_ref[0])
    out_ref[0] = total.astype(BF16)


def finish(rows, own, b_ext, coef, above, below):
    parts, nodes, width = own.shape
    slots = rows.shape[1]
    columns = b_ext.shape[2]
    part = lambda a: pl.BlockSpec((1, a, width), lambda i: (i, 0, 0))
    return pl.pallas_call(
        final_kernel,
        grid=(parts,),
        in_specs=[
            whole(rows),
            part(nodes),
            pl.BlockSpec((1, nodes, columns), lambda i: (i, 0, 0)),
            pl.BlockSpec((1, columns, width), lambda i: (i // 2, 0, 0)),
            part(slots),
            part(slots),
        ],
        out_specs=part(nodes),
        out_shape=jax.ShapeDtypeStruct((parts, nodes, width), BF16),
        scratch_shapes=[vmem((nodes, 2 * slots), BF16)],
        name="finish",
    )(rows, own, b_ext, coef, above, below)


def per_device(residual, patch_inv, coarse_basis, coarse_inv, patch_slots, send_rows, coarse_block):
    waves, _, nodes, width = residual.shape
    patches = patch_inv.shape[0]
    size = coarse_basis.shape[3]
    slots = send_rows.shape[2]
    ext = nodes + 2 * slots
    owners = lax.axis_size(AXES)
    halves = width // LANES
    groups = owners // (waves * halves)
    per_group = size // groups
    assert groups * waves * halves == owners and per_group * groups == size
    rows = patches * per_group
    padded = -(-(rows + patches) // 8) * 8
    x4 = residual.reshape(2 * waves, nodes, width)
    send = send_rows[0]

    up, down = select_rows(x4, send)
    below = passed_along(up, AXES, 1)
    above = passed_along(down, AXES, -1)
    basis_t = jnp.swapaxes(coarse_basis, 2, 3)
    pos, rest_ids, crem, y, r_own, bt_rem, b_ext = prepare(patch_slots, basis_t, x4, ext)
    count = lax.axis_size("coarse")
    inverses = jnp.stack(
        [coarse_inv] + [passed_along(coarse_inv, "coarse", -k) for k in range(1, count)]
    )
    place = lax.axis_index("coarse").astype(jnp.int32).reshape(1)

    sent = restrict(coarse_block, r_own, bt_rem, below, above, owners, per_group, padded)
    got = lax.all_to_all(sent, AXES, 0, 0, tiled=True)
    half = patches // 2
    first = local_products(pos, x4, y, crem, below, above, patch_inv, 0, half)
    sums = owner_sums(got, patches, per_group)
    mine = lax.all_to_all(sums, AXES, 0, 0, tiled=True)
    second = local_products(pos, x4, y, crem, below, above, patch_inv, half, patches - half)
    own, margin = scatter(rest_ids, [first, second], nodes, ext)
    coef, low, high = coefficients(
        coarse_block, place, mine, inverses, b_ext, margin, nodes, per_group
    )
    back_above = passed_along(low, AXES, -1)
    back_below = passed_along(high, AXES, 1)
    out = finish(send, own, b_ext, coef, back_above, back_below)
    return out.reshape(residual.shape)


def solution(mesh):
    placed = (
        P(None, None, AXES, None),
        P(AXES, None, None, None),
        P(AXES, None, None, None),
        P("coarse", None, None, None),
        P(AXES, None),
        P(AXES, None, None),
        P(AXES),
    )
    return jax.shard_map(
        per_device,
        mesh=mesh,
        in_specs=placed,
        out_specs=P(None, None, AXES, None),
        check_vma=False,
    )
```

```python
import functools

import jax
import jax.numpy as jnp
from jax import lax
from jax.experimental import pallas as pl
from jax.experimental.pallas import tpu as pltpu
from jax.sharding import PartitionSpec as P


AXES = ("patch", "coarse")
LANES = 128
MIB = 1 << 20
F32 = jnp.float32
BF16 = jnp.bfloat16


def passed_along(value, axis, steps):
    count = lax.axis_size(axis)
    pairs = [(source, (source + steps) % count) for source in range(count)]
    return lax.ppermute(value, axis, pairs)


def dot(a, b):
    return jnp.dot(a, b, preferred_element_type=F32)


def beside(parts):
    return jnp.concatenate(parts, axis=1)


def dot_in_halves(a_ref, b):
    half = b.shape[0] // 2
    return dot(a_ref[:, :half], b[:half]) + dot(a_ref[:, half:], b[half:])


def as_column(row):
    return jnp.transpose(jnp.broadcast_to(row, (LANES, row.shape[1])))


def iota(shape, axis):
    return lax.broadcasted_iota(jnp.int32, shape, axis)


def one_hot_rows(column, width, start=0):
    rows = column.shape[0]
    parts = [
        (column == (iota((rows, LANES), 1) + (start + t)).astype(F32)).astype(F32).astype(BF16)
        for t in range(0, width, LANES)
    ]
    return jnp.concatenate(parts, axis=1)


def vmem(shape, dtype):
    return pltpu.VMEM(shape, dtype)


def resident(array):
    return pltpu.with_memory_space_constraint(array, pltpu.VMEM)


def call(kernel, limit, smem, far, near, far_out, near_out, scratch=()):
    spaces = [pltpu.SMEM] * len(smem) + [pltpu.HBM] * len(far) + [pltpu.VMEM] * len(near)
    out_spaces = [pltpu.HBM] * len(far_out) + [pltpu.VMEM] * len(near_out)
    return pl.pallas_call(
        kernel,
        in_specs=[pl.BlockSpec(memory_space=m) for m in spaces],
        out_specs=[pl.BlockSpec(memory_space=m) for m in out_spaces],
        out_shape=[pltpu.HBM(*o) for o in far_out] + [vmem(*o) for o in near_out],
        scratch_shapes=list(scratch),
        compiler_params=pltpu.CompilerParams(vmem_limit_bytes=limit * MIB),
    )(
        *smem,
        *[pltpu.with_memory_space_constraint(a, pltpu.HBM) for a in far],
        *[resident(a) for a in near],
    )


def copy(source, target, sem):
    moved = pltpu.make_async_copy(source, target, sem)
    moved.start()
    return moved


def select_kernel(
    x_hbm, rows_hbm, slots_hbm, up_ref, down_ref, x_ref, slots_ref,
    rows_ref, arrived,
):
    slots = rows_ref.shape[1]
    parts, nodes, _ = x_ref.shape
    small = pltpu.make_async_copy(rows_hbm, rows_ref, arrived.at[parts])
    copies = [pltpu.make_async_copy(x_hbm.at[k], x_ref.at[k], arrived.at[k]) for k in range(parts)]
    later = pltpu.make_async_copy(slots_hbm, slots_ref, arrived.at[parts + 1])
    for copy in [small] + copies + [later]:
        copy.start()
    small.wait()
    pick = jnp.concatenate(
        [one_hot_rows(as_column(rows_ref[b : b + 1, :].astype(F32)), nodes) for b in range(2)], axis=0
    )
    width = x_ref.shape[2]
    for k in range(0, parts, 2):
        copies[k].wait()
        copies[k + 1].wait()
        got = dot(pick, beside([x_ref[k], x_ref[k + 1]])).astype(BF16)
        for j in range(2):
            up_ref[k + j] = got[:slots, j * width : (j + 1) * width]
            down_ref[k + j] = got[slots:, j * width : (j + 1) * width]
    later.wait()


def select_rows(x4, rows, patch_slots):
    parts, _, width = x4.shape
    slots = rows.shape[1]
    margin = vmem((parts, slots, width), BF16)
    kept = [vmem(a.shape, a.dtype) for a in (x4, patch_slots)]
    return pl.pallas_call(
        select_kernel,
        in_specs=[pl.BlockSpec(memory_space=pltpu.HBM)] * 3,
        out_specs=[pl.BlockSpec(memory_space=pltpu.VMEM)] * 4,
        out_shape=[margin, margin] + kept,
        scratch_shapes=[vmem(rows.shape, rows.dtype), pltpu.SemaphoreType.DMA((parts + 2,))],
        compiler_params=pltpu.CompilerParams(vmem_limit_bytes=6 * MIB),
        name="select",
    )(*[pltpu.with_memory_space_constraint(a, pltpu.HBM) for a in (x4, rows, patch_slots)])


def prep_kernel(
    basis_hbm, slots_ref, x_ref,
    crem_hbm, y_hbm, bext_hbm, pos_ref, rest_ref, r_ref, btrem_ref,
    ccat, bt, basis_ref, y_ref, bext_ref, sems,
):
    basis_in = copy(basis_hbm, basis_ref, sems.at[0])
    patches, patch_nodes = slots_ref.shape
    waves, width = basis_ref.shape[1], basis_ref.shape[2]
    parts, nodes, _ = x_ref.shape
    core = nodes // patches
    rest = patch_nodes - core
    ext = ccat.shape[1]
    slots = slots_ref[...].astype(F32)
    first = (iota((patches, patch_nodes), 0) * core).astype(F32)
    local = slots - first
    outside = (local < 0.0) | (local >= float(core))
    before = iota((patch_nodes, patch_nodes), 0) < iota((patch_nodes, patch_nodes), 1)
    rank = dot(outside.astype(F32).astype(BF16), before.astype(F32).astype(BF16))
    pos = jnp.where(outside, rank + float(core), local)
    pos_ref[...] = pos
    basis_in.wait()
    for p in range(patches):
        prow = pos[p : p + 1, :]
        srow = slots[p : p + 1, :]
        permute = one_hot_rows(as_column(prow), patch_nodes)
        basis = jnp.concatenate(
            [
                basis_ref[p, w, :, q * patch_nodes : (q + 1) * patch_nodes]
                for w in range(waves)
                for q in range(2)
            ],
            axis=0,
        )
        moved = dot(basis, permute).astype(BF16)
        hit = prow == (iota((rest, patch_nodes), 0) + core).astype(F32)
        ids = jnp.sum(
            jnp.where(hit, jnp.broadcast_to(srow, hit.shape), 0.0), axis=1, keepdims=True
        )
        ids = jnp.broadcast_to(ids, (rest, LANES))
        rest_ref[:, p * rest : (p + 1) * rest] = jnp.transpose(ids)[0:8]
        pick = one_hot_rows(ids, ext)
        ccat[p * rest : (p + 1) * rest, :] = pick
        spread = dot(moved[:, core:], pick).astype(BF16)
        for k in range(parts):
            rows = slice(k * width, (k + 1) * width)
            here = slice(p * width, (p + 1) * width)
            bt[k, here, :] = spread[rows]
            bt[k, here, p * core : (p + 1) * core] = (
                spread[rows, p * core : (p + 1) * core] + moved[rows, :core]
            )
    sent = [copy(ccat.at[:, pl.ds(nodes, ext - nodes)], crem_hbm, sems.at[1])]
    for k in range(parts):
        btrem_ref[k] = bt[k, :, nodes:]
        bext_ref[k] = jnp.transpose(bt[k])
        sent.append(copy(bext_ref.at[k], bext_hbm.at[k], sems.at[3 + 2 * k]))
    for k in range(0, parts, 2):
        both = dot(ccat[:, :nodes], beside([x_ref[k], x_ref[k + 1]])).astype(BF16)
        for j in range(2):
            y_ref[k + j] = both[:, j * x_ref.shape[2] : (j + 1) * x_ref.shape[2]]
    for k in range(parts):
        sent.append(copy(y_ref.at[k], y_hbm.at[k], sems.at[2 + 2 * k]))
    for w in range(waves):
        r_ref[w] = sum(dot(bt[k, :, :nodes], x_ref[k]) for k in (2 * w, 2 * w + 1))
    for moved in sent:
        moved.wait()


def prepare(slots, basis_t, x4, ext):
    parts, nodes, width = x4.shape
    patches, patch_nodes = slots.shape
    rest = patch_nodes - nodes // patches
    columns = patches * basis_t.shape[2]
    y = ((parts, patches * rest, width), BF16)
    b_ext = ((parts, ext, columns), BF16)
    return call(
        prep_kernel,
        12,
        [],
        [basis_t],
        [slots, x4],
        [((patches * rest, ext - nodes), BF16), y, b_ext],
        [
            ((patches, patch_nodes), F32),
            ((8, patches * rest), F32),
            ((parts // 2, columns, width), F32),
            ((parts, columns, ext - nodes), BF16),
        ],
        [
            vmem((patches * rest, ext), BF16),
            vmem((parts, columns, ext), BF16),
            vmem(basis_t.shape, BF16),
            vmem(*y),
            vmem(*b_ext),
            pltpu.SemaphoreType.DMA((2 + 2 * parts,)),
        ],
    )


def owner_order(columns, patches, width, per_group):
    rows = patches * per_group
    i = iota((columns, columns), 0)
    j = iota((columns, columns), 1)
    source = ((i % rows) // per_group) * width + (i // rows) * per_group + i % per_group
    return (source == j).astype(F32).astype(BF16)


def restrict_kernel(per_group, block_ref, r_ref, btrem_ref, below_ref, above_ref, inv_ref, out_ref):
    waves, columns, width = r_ref.shape
    patches = block_ref.shape[0]
    slots = below_ref.shape[1]
    rows = patches * per_group
    groups = columns // rows
    halves = width // LANES
    order = owner_order(columns, patches, columns // patches, per_group)
    tail = out_ref.shape[1] - rows
    keys = jnp.zeros((tail, LANES), F32)
    for p in range(patches):
        keys = jnp.where(iota((tail, LANES), 0) == p, block_ref[p].astype(F32), keys)
    for w in range(waves):
        total = r_ref[w]
        for q in range(2):
            k = 2 * w + q
            total = total + dot(btrem_ref[k, :, :slots], below_ref[k])
            total = total + dot(btrem_ref[k, :, slots:], above_ref[k])
        moved = dot(order, total.astype(BF16)).astype(BF16)
        for g in range(groups):
            last = (keys + inv_ref[w * groups + g]).astype(BF16)
            for h in range(halves):
                owner = (w * groups + g) * halves + h
                out_ref[owner, :rows, :] = moved[g * rows : (g + 1) * rows, h * LANES : (h + 1) * LANES]
                out_ref[owner, rows:, :] = last


def restrict(block, r_own, bt_rem, below, above, inv_rows, owners, per_group, padded):
    out = ((owners, padded, LANES), BF16)
    return call(
        functools.partial(restrict_kernel, per_group),
        3,
        [block],
        [],
        [r_own, bt_rem, below, above, inv_rows],
        [],
        [out],
    )[0]


def inverse_rows(coarse_inv, patches, per_group, tail, share):
    blocks, waves, size, _ = coarse_inv.shape
    count = lax.axis_size("patch")
    padded = jnp.pad(coarse_inv, ((0, count * share - blocks), (0, 0), (0, 0), (0, 0)))
    mine = lax.dynamic_slice_in_dim(padded, lax.axis_index("patch") * share, share, 0)
    mine = mine.reshape(share, waves, size, size // per_group, per_group)
    mine = mine.transpose(1, 3, 0, 4, 2).reshape(waves * (size // per_group), share, per_group * size)
    edges = ((0, 0), (patches, tail - patches - share), (0, LANES - per_group * size))
    return jnp.pad(mine.astype(F32), edges)


def sums_kernel(per_group, patches, coarse_count, blocks, share, got_ref, out_ref, data, tags):
    owners, padded, _ = got_ref.shape
    rows = patches * per_group
    tail = padded - rows
    for s in range(owners):
        data[s * rows : (s + 1) * rows, :] = got_ref[s, :rows, :].astype(F32)
        tags[s * tail : (s + 1) * tail, :] = got_ref[s, rows:, :].astype(F32)
    tag = tags[...].astype(BF16)
    count = owners * rows
    i = iota((count, owners * tail), 0)
    j = iota((count, owners * tail), 1)
    wanted = (i // rows) * tail + (i % rows) // per_group
    keys = dot((wanted == j).astype(F32).astype(BF16), tag)
    keys = keys * float(per_group) + (iota((count, LANES), 0) % per_group).astype(F32)
    key_row = jnp.transpose(keys)[0:1, :]
    column = jnp.concatenate([keys] * (count // LANES), axis=1)
    same = (column == key_row).astype(F32).astype(BF16)
    data[...] = dot(same, data[...].astype(BF16))

    pairs = owners * patches
    i = iota((pairs, owners * tail), 0)
    j = iota((pairs, owners * tail), 1)
    named = dot(((i // patches) * tail + i % patches == j).astype(F32).astype(BF16), tag)
    source, place = j // tail, j % tail - patches
    block = (source // coarse_count) * share + place
    held = (place >= 0) & (place < share) & (block < blocks)
    block = jnp.where(held, (source % coarse_count) * blocks + block, -1).astype(F32)
    if owners * tail >= LANES:
        named = jnp.concatenate([named] * (owners * tail // LANES), axis=1)
    tags[0:pairs, :] = dot((named == block).astype(F32).astype(BF16), tag)
    extra = out_ref.shape[1] - rows - patches
    for s in range(owners):
        out_ref[s, :rows, :] = data[s * rows : (s + 1) * rows, :].astype(BF16)
        last = tags[s * patches : (s + 1) * patches, :]
        if extra:
            last = jnp.concatenate([last, jnp.zeros((extra, LANES), F32)], axis=0)
        out_ref[s, rows:, :] = last.astype(BF16)


def owner_sums(got, patches, per_group, blocks, share):
    owners, padded, _ = got.shape
    rows = patches * per_group
    back = -(-(rows + patches) // 8) * 8
    out = ((owners, back, LANES), BF16)
    return call(
        functools.partial(
            sums_kernel, per_group, patches, lax.axis_size("coarse"), blocks, share
        ),
        6,
        [],
        [],
        [got],
        [],
        [out],
        [
            vmem((owners * rows, LANES), F32),
            vmem((owners * (padded - rows), LANES), F32),
        ],
    )[0]


def local_kernel(
    first, inv_hbm, x_hbm, y_hbm, crem_hbm, below_hbm, above_hbm, pos_ref,
    local_hbm, rest_hbm,
    g, inv_ref, x_ref, y_ref, crem_ref, far_ref, local_ref, rest_ref, order_ref, back_ref,
    sems, inv_sems, out_sems,
):
    parts, rows, width = x_ref.shape
    count, waves = inv_ref.shape[:2]
    patch_nodes = pos_ref.shape[1]
    core = rows // count
    rest = patch_nodes - core
    slots = below_hbm.shape[1]
    mine = pl.ds(first * rest, count * rest)
    small = [
        copy(crem_hbm.at[mine], crem_ref, sems.at[0]),
        copy(below_hbm, far_ref.at[:, pl.ds(0, slots)], sems.at[1]),
        copy(above_hbm, far_ref.at[:, pl.ds(slots, slots)], sems.at[2]),
        copy(y_hbm.at[:, mine], y_ref, sems.at[3]),
        copy(x_hbm.at[:, pl.ds(first * core, rows)], x_ref, sems.at[4]),
    ]
    inverses = {
        (i, w): copy(inv_hbm.at[first + i, w], inv_ref.at[i, w], inv_sems.at[i * waves + w])
        for i in range(count)
        for w in range(waves)
    }
    for i in range(count):
        prow = pos_ref[first + i : first + i + 1, :]
        order_ref[i] = one_hot_rows(as_column(prow), patch_nodes)
        places = (iota((rest, patch_nodes), 0) + core).astype(F32)
        back_ref[i] = (prow == places).astype(F32).astype(BF16)
    for moved in small:
        moved.wait()
    sent = []
    for i in range(count):
        here = slice(i * rest, (i + 1) * rest)
        for k in range(0, parts, 2):
            far = dot(crem_ref[here, :], beside([far_ref[k], far_ref[k + 1]]))
            other = beside([y_ref[k, here, :], y_ref[k + 1, here, :]]) + far.astype(BF16)
            rows = slice(i * core, (i + 1) * core)
            mine = beside([x_ref[k, rows, :], x_ref[k + 1, rows, :]])
            moved = dot(order_ref[i], jnp.concatenate([mine, other], axis=0)).astype(BF16)
            for j in range(2):
                at = (k + j) * patch_nodes
                g[at : at + patch_nodes, :] = moved[:, j * width : (j + 1) * width]
        for w in range(waves):
            inverses[i, w].wait()
        for w in range(waves):
            terms = g[2 * w * patch_nodes : 2 * (w + 1) * patch_nodes, :]
            local_ref[i, w] = dot_in_halves(inv_ref.at[i, w], terms).astype(BF16)
        for w in range(waves):
            pair = beside([local_ref[i, w, :patch_nodes, :], local_ref[i, w, patch_nodes:, :]])
            got = dot(back_ref[i], pair).astype(BF16)
            for j in range(2):
                rest_ref[2 * w + j, here, :] = got[:, j * width : (j + 1) * width]
            sent.append(copy(local_ref.at[i, w], local_hbm.at[i, w], out_sems.at[i, w]))
    sent.append(copy(rest_ref, rest_hbm, sems.at[0]))
    for moved in sent:
        moved.wait()


def local_products(pos, x4, y, crem, below, above, patch_inv, first, count):
    parts, nodes, width = x4.shape
    patches, patch_nodes = pos.shape
    core = nodes // patches
    rest = patch_nodes - core
    waves = patch_inv.shape[1]
    local = ((count, waves, 2 * patch_nodes, width), BF16)
    others = ((parts, count * rest, width), BF16)
    return call(
        functools.partial(local_kernel, first),
        24,
        [],
        [patch_inv, x4, y, crem, below, above],
        [pos],
        [local, others],
        [],
        [
            vmem((parts * patch_nodes, width), BF16),
            vmem((count,) + patch_inv.shape[1:], BF16),
            vmem((parts, count * core, width), BF16),
            vmem(*others),
            vmem((count * rest, crem.shape[1]), BF16),
            vmem((parts, crem.shape[1], width), BF16),
            vmem(*local),
            vmem(*others),
            vmem((count, patch_nodes, patch_nodes), BF16),
            vmem((count, rest, patch_nodes), BF16),
            pltpu.SemaphoreType.DMA((5,)),
            pltpu.SemaphoreType.DMA((count * waves,)),
            pltpu.SemaphoreType.DMA((count, waves)),
        ],
    )


def coef_kernel(
    per_group, patches, bext_hbm, *refs
):
    *other_hbm, sums_ref, rest_ref, coef_ref, low_ref, high_ref = refs[:-5]
    gathered, inverses, brem_ref, other_ref, sems = refs[-5:]
    slots = low_ref.shape[1]
    nodes = bext_hbm.shape[1] - 2 * slots
    arriving = [copy(bext_hbm.at[:, pl.ds(nodes, 2 * slots)], brem_ref, sems.at[0])]
    start = 0
    for i, other in enumerate(other_hbm):
        place = pl.ds(start, other.shape[1])
        arriving.append(copy(other, other_ref.at[:, place], sems.at[1 + i]))
        start += other.shape[1]
    waves, columns, width = coef_ref.shape
    size = columns // patches
    rows = patches * per_group
    groups = columns // rows
    halves = width // LANES
    held = groups * patches
    i = iota((columns, held), 0)
    j = iota((columns, held), 1)
    grow = ((i // rows) * patches + (i % rows) // per_group == j).astype(F32).astype(BF16)
    i = iota((columns, LANES), 0)
    j = iota((columns, LANES), 1)
    in_lanes = j // size == i % per_group
    fold = (iota((LANES, columns), 0) % size == iota((LANES, columns), 1) % size)
    fold = fold.astype(F32).astype(BF16)
    i = iota((columns, columns), 0)
    j = iota((columns, columns), 1)
    in_patch = j // size == (i % rows) // per_group
    ids = rest_ref[0:1, :]
    reach = (2 * slots, ids.shape[1])
    spread = (ids == (iota(reach, 0) + nodes).astype(F32)).astype(F32).astype(BF16)
    for w in range(waves):
        for g in range(groups):
            for h in range(halves):
                owner = (w * groups + g) * halves + h
                gathered[g * rows : (g + 1) * rows, h * LANES : (h + 1) * LANES] = sums_ref[
                    owner, :rows, :
                ].astype(F32)
            inverses[g * patches : (g + 1) * patches, :] = sums_ref[
                (w * groups + g) * halves, rows : rows + patches, :
            ].astype(F32)
        grown = dot(grow, inverses[...].astype(BF16))
        folded = dot(jnp.where(in_lanes, grown, 0.0).astype(BF16), fold)
        inverse = jnp.transpose(jnp.where(in_patch, folded, 0.0)).astype(BF16)
        coef = dot(inverse, gathered[...].astype(BF16)).astype(BF16)
        coef_ref[w] = coef
        if w == 0:
            for moved in arriving:
                moved.wait()
        for q in range(2):
            k = 2 * w + q
            margin = (dot(spread, other_ref[k]) + dot(brem_ref[k], coef)).astype(BF16)
            low_ref[k] = margin[:slots]
            high_ref[k] = margin[slots:]


def coefficients(sums, b_ext, rest_ids, others, patches, slots, per_group):
    parts, _, columns = b_ext.shape
    width = others[0].shape[2]
    groups = columns // (patches * per_group)
    margin = ((parts, slots, width), BF16)
    return call(
        functools.partial(coef_kernel, per_group, patches),
        6,
        [],
        [b_ext] + others,
        [sums, rest_ids],
        [],
        [((parts // 2, columns, width), BF16), margin, margin],
        [
            vmem((columns, width), F32),
            vmem((groups * patches, LANES), F32),
            vmem((parts, 2 * slots, columns), BF16),
            vmem((parts, rest_ids.shape[1], width), BF16),
            pltpu.SemaphoreType.DMA((1 + len(others),)),
        ],
    )


def own_kernel(bext_hbm, *refs):
    *pairs, rest_ref, pos_ref, coef_ref, out_ref, bown_ref, local_ref, other_ref, sems = refs
    half = len(pairs) // 2
    parts, nodes, _ = out_ref.shape
    patches, patch_nodes = pos_ref.shape
    core = nodes // patches
    arriving = []
    for k in range(parts):
        moves = [(bext_hbm.at[k, pl.ds(0, nodes)], bown_ref.at[k])]
        start = 0
        for a in pairs[half:]:
            moves.append((a.at[k], other_ref.at[k, pl.ds(start, a.shape[1])]))
            start += a.shape[1]
        start = 0
        terms = pl.ds((k % 2) * patch_nodes, patch_nodes)
        for a in pairs[:half]:
            here = pl.ds(start, a.shape[0])
            moves.append((a.at[:, k // 2, terms], local_ref.at[k, here]))
            start += a.shape[0]
        arriving.append([copy(a, b, sems.at[k, i]) for i, (a, b) in enumerate(moves)])
    ids = rest_ref[0:1, :]
    shape = (nodes, ids.shape[1])
    spread = (ids == iota(shape, 0).astype(F32)).astype(F32).astype(BF16)
    places = iota((core, patch_nodes), 0).astype(F32)
    backs = [
        (pos_ref[p : p + 1, :] == places).astype(F32).astype(BF16) for p in range(patches)
    ]
    width = out_ref.shape[2]
    for k in range(0, parts, 2):
        for moved in arriving[k] + arriving[k + 1]:
            moved.wait()
        total = dot(spread, beside([other_ref[k], other_ref[k + 1]]))
        cores = [
            dot(backs[p], beside([local_ref[k, p], local_ref[k + 1, p]])) for p in range(patches)
        ]
        total = total + jnp.concatenate(cores, axis=0)
        for j in range(2):
            coarse = dot(bown_ref[k + j], coef_ref[(k + j) // 2])
            out_ref[k + j] = total[:, j * width : (j + 1) * width] + coarse


def own_rows(b_ext, coef, rest_ids, pos, locals_, others, nodes):
    parts, _, columns = b_ext.shape
    width = coef.shape[2]
    return call(
        own_kernel,
        20,
        [],
        [b_ext] + locals_ + others,
        [rest_ids, pos, coef],
        [],
        [((parts, nodes, width), F32)],
        [
            vmem((parts, nodes, columns), BF16),
            vmem((parts,) + pos.shape + (width,), BF16),
            vmem((parts, rest_ids.shape[1], width), BF16),
            pltpu.SemaphoreType.DMA((parts, 1 + len(locals_) + len(others))),
        ],
    )[0]


def final_kernel(rows_ref, own_ref, above_ref, below_ref, out_ref, spread):
    slots = rows_ref.shape[1]
    nodes = own_ref.shape[1]
    k = pl.program_id(0)

    @pl.when(k == 0)
    def _():
        for b in range(2):
            ids = rows_ref[b : b + 1, :].astype(F32)
            spread[:, b * slots : (b + 1) * slots] = (
                (ids == iota((nodes, slots), 0).astype(F32)).astype(F32).astype(BF16)
            )

    back = jnp.concatenate([above_ref[k], below_ref[k]], axis=0)
    out_ref[0] = (own_ref[k] + dot(spread[...], back)).astype(BF16)


def finish(rows, own, above, below):
    parts, nodes, width = own.shape
    spec = pl.BlockSpec(memory_space=pltpu.VMEM)
    return pl.pallas_call(
        final_kernel,
        grid=(parts,),
        in_specs=[spec] * 4,
        out_specs=pl.BlockSpec((1, nodes, width), lambda i: (i, 0, 0)),
        out_shape=jax.ShapeDtypeStruct((parts, nodes, width), BF16),
        scratch_shapes=[vmem((nodes, 2 * rows.shape[1]), BF16)],
        compiler_params=pltpu.CompilerParams(vmem_limit_bytes=8 * MIB),
        name="finish",
    )(*[resident(a) for a in (rows, own, above, below)])


def per_device(residual, patch_inv, coarse_basis, coarse_inv, patch_slots, send_rows, coarse_block):
    waves, _, nodes, width = residual.shape
    patches = patch_inv.shape[0]
    size = coarse_basis.shape[3]
    slots = send_rows.shape[2]
    ext = nodes + 2 * slots
    owners = lax.axis_size(AXES)
    halves = width // LANES
    groups = owners // (waves * halves)
    per_group = size // groups
    assert groups * waves * halves == owners and per_group * groups == size
    blocks = coarse_inv.shape[0]
    share = -(-blocks // lax.axis_size("patch"))
    rows = patches * per_group
    padded = -(-(rows + patches + share) // 8) * 8
    half = patches // 2
    send = send_rows[0]
    basis_t = jnp.swapaxes(coarse_basis, 2, 3)

    x_all = residual.reshape(2 * waves, nodes, width)
    up, down, x4, slots_v = select_rows(x_all, send, patch_slots)
    below = passed_along(up, AXES, 1)
    above = passed_along(down, AXES, -1)
    crem, y, b_ext, pos, rest_ids, r_own, bt_rem = prepare(slots_v, basis_t, x4, ext)
    inv_rows = inverse_rows(coarse_inv, patches, per_group, padded - rows, share)
    sent = restrict(coarse_block, r_own, bt_rem, below, above, inv_rows, owners, per_group, padded)
    got = lax.all_to_all(sent, AXES, 0, 0, tiled=True)
    local_a, rest_a = local_products(pos, x_all, y, crem, below, above, patch_inv, 0, half)
    sums = owner_sums(got, patches, per_group, blocks, share)
    mine = lax.all_to_all(sums, AXES, 0, 0, tiled=True)
    local_b, rest_b = local_products(
        pos, x_all, y, crem, below, above, patch_inv, half, patches - half
    )
    coef, low, high = coefficients(
        mine, b_ext, rest_ids, [rest_a, rest_b], patches, slots, per_group
    )
    back_above = passed_along(low, AXES, -1)
    back_below = passed_along(high, AXES, 1)
    own = own_rows(b_ext, coef, rest_ids, pos, [local_a, local_b], [rest_a, rest_b], nodes)
    out = finish(send, own, back_above, back_below)
    return out.reshape(residual.shape)


def solution(mesh):
    placed = (
        P(None, None, AXES, None),
        P(AXES, None, None, None),
        P(AXES, None, None, None),
        P("coarse", None, None, None),
        P(AXES, None),
        P(AXES, None, None),
        P(AXES),
    )
    return jax.shard_map(
        per_device,
        mesh=mesh,
        in_specs=placed,
        out_specs=P(None, None, AXES, None),
        check_vma=False,
    )
```

```python
import functools

import jax
import jax.numpy as jnp
from jax import lax
from jax.experimental import pallas as pl
from jax.experimental.pallas import tpu as pltpu
from jax.sharding import PartitionSpec as P


AXES = ("patch", "coarse")
LANES = 128
MIB = 1 << 20
F32 = jnp.float32
BF16 = jnp.bfloat16


def passed_along(value, axis, steps):
    count = lax.axis_size(axis)
    pairs = [(source, (source + steps) % count) for source in range(count)]
    return lax.ppermute(value, axis, pairs)


def dot(a, b):
    return jnp.dot(a, b, preferred_element_type=F32)


def beside(parts):
    return jnp.concatenate(parts, axis=1)


def dot_in_halves(a_ref, b):
    half = b.shape[0] // 2
    return dot(a_ref[:, :half], b[:half]) + dot(a_ref[:, half:], b[half:])


def as_column(row):
    return jnp.transpose(jnp.broadcast_to(row, (LANES, row.shape[1])))


def iota(shape, axis):
    return lax.broadcasted_iota(jnp.int32, shape, axis)


def one_hot_rows(column, width, start=0):
    rows = column.shape[0]
    parts = [
        (column == (iota((rows, LANES), 1) + (start + t)).astype(F32)).astype(F32).astype(BF16)
        for t in range(0, width, LANES)
    ]
    return jnp.concatenate(parts, axis=1)


def vmem(shape, dtype):
    return pltpu.VMEM(shape, dtype)


def resident(array):
    return pltpu.with_memory_space_constraint(array, pltpu.VMEM)


def call(kernel, limit, smem, far, near, far_out, near_out, scratch=()):
    spaces = [pltpu.SMEM] * len(smem) + [pltpu.HBM] * len(far) + [pltpu.VMEM] * len(near)
    out_spaces = [pltpu.HBM] * len(far_out) + [pltpu.VMEM] * len(near_out)
    return pl.pallas_call(
        kernel,
        in_specs=[pl.BlockSpec(memory_space=m) for m in spaces],
        out_specs=[pl.BlockSpec(memory_space=m) for m in out_spaces],
        out_shape=[pltpu.HBM(*o) for o in far_out] + [vmem(*o) for o in near_out],
        scratch_shapes=list(scratch),
        compiler_params=pltpu.CompilerParams(vmem_limit_bytes=limit * MIB),
    )(
        *smem,
        *[pltpu.with_memory_space_constraint(a, pltpu.HBM) for a in far],
        *[resident(a) for a in near],
    )


def copy(source, target, sem, priority=0):
    moved = pltpu.make_async_copy(source, target, sem)
    moved.start(priority=priority)
    return moved


def select_kernel(
    x_hbm, rows_hbm, slots_hbm, up_ref, down_ref, x_ref, slots_ref,
    rows_ref, arrived,
):
    slots = rows_ref.shape[1]
    parts, nodes, _ = x_ref.shape
    small = pltpu.make_async_copy(rows_hbm, rows_ref, arrived.at[parts])
    copies = [pltpu.make_async_copy(x_hbm.at[k], x_ref.at[k], arrived.at[k]) for k in range(parts)]
    later = pltpu.make_async_copy(slots_hbm, slots_ref, arrived.at[parts + 1])
    for copy in [small] + copies + [later]:
        copy.start()
    small.wait()
    pick = jnp.concatenate(
        [one_hot_rows(as_column(rows_ref[b : b + 1, :].astype(F32)), nodes) for b in range(2)], axis=0
    )
    width = x_ref.shape[2]
    for k in range(0, parts, 2):
        copies[k].wait()
        copies[k + 1].wait()
        got = dot(pick, beside([x_ref[k], x_ref[k + 1]])).astype(BF16)
        for j in range(2):
            up_ref[k + j] = got[:slots, j * width : (j + 1) * width]
            down_ref[k + j] = got[slots:, j * width : (j + 1) * width]
    later.wait()


def select_rows(x4, rows, patch_slots):
    parts, _, width = x4.shape
    slots = rows.shape[1]
    margin = vmem((parts, slots, width), BF16)
    kept = [vmem(a.shape, a.dtype) for a in (x4, patch_slots)]
    return pl.pallas_call(
        select_kernel,
        in_specs=[pl.BlockSpec(memory_space=pltpu.HBM)] * 3,
        out_specs=[pl.BlockSpec(memory_space=pltpu.VMEM)] * 4,
        out_shape=[margin, margin] + kept,
        scratch_shapes=[vmem(rows.shape, rows.dtype), pltpu.SemaphoreType.DMA((parts + 2,))],
        compiler_params=pltpu.CompilerParams(vmem_limit_bytes=6 * MIB),
        name="select",
    )(*[pltpu.with_memory_space_constraint(a, pltpu.HBM) for a in (x4, rows, patch_slots)])


def prep_kernel(
    per_group, share, place_ref, basis_hbm, inv_hbm, slots_ref, x_ref,
    crem_hbm, y_hbm, bext_hbm, pos_ref, rest_ref, r_ref, btrem_ref, lines_ref,
    ccat, bt, basis_ref, y_ref, bext_ref, order_ref, inv_ref, square, sems,
):
    basis_in = copy(basis_hbm, basis_ref, sems.at[0])
    held = jnp.minimum(place_ref[0] * share, inv_hbm.shape[0] - share)
    inv_in = copy(inv_hbm.at[pl.ds(held, share)], inv_ref, sems.at[4])
    patches, patch_nodes = slots_ref.shape
    waves, width = basis_ref.shape[1], basis_ref.shape[2]
    parts, nodes, _ = x_ref.shape
    core = nodes // patches
    rest = patch_nodes - core
    ext = ccat.shape[1]
    slots = slots_ref[...].astype(F32)
    first = (iota((patches, patch_nodes), 0) * core).astype(F32)
    local = slots - first
    outside = (local < 0.0) | (local >= float(core))
    before = iota((patch_nodes, patch_nodes), 0) < iota((patch_nodes, patch_nodes), 1)
    rank = dot(outside.astype(F32).astype(BF16), before.astype(F32).astype(BF16))
    pos = jnp.where(outside, rank + float(core), local)
    pos_ref[...] = pos
    for p in range(patches):
        prow = pos[p : p + 1, :]
        order_ref[p] = one_hot_rows(as_column(prow), patch_nodes)
        hit = prow == (iota((rest, patch_nodes), 0) + core).astype(F32)
        ids = jnp.sum(
            jnp.where(hit, jnp.broadcast_to(slots[p : p + 1, :], hit.shape), 0.0),
            axis=1,
            keepdims=True,
        )
        ids = jnp.broadcast_to(ids, (rest, LANES))
        rest_ref[:, p * rest : (p + 1) * rest] = jnp.transpose(ids)[0:8]
        ccat[p * rest : (p + 1) * rest, :] = one_hot_rows(ids, ext)
    basis_in.wait()
    for p in range(patches):
        basis = jnp.concatenate(
            [
                basis_ref[p, w, :, q * patch_nodes : (q + 1) * patch_nodes]
                for w in range(waves)
                for q in range(2)
            ],
            axis=0,
        )
        moved = dot(basis, order_ref[p]).astype(BF16)
        spread = dot(moved[:, core:], ccat[p * rest : (p + 1) * rest, :]).astype(BF16)
        for k in range(parts):
            rows = slice(k * width, (k + 1) * width)
            here = slice(p * width, (p + 1) * width)
            bt[k, here, :] = spread[rows]
            bt[k, here, p * core : (p + 1) * core] = (
                spread[rows, p * core : (p + 1) * core] + moved[rows, :core]
            )
    for k in range(0, parts, 2):
        both = dot(ccat[:, :nodes], beside([x_ref[k], x_ref[k + 1]])).astype(BF16)
        for j in range(2):
            y_ref[k + j] = both[:, j * x_ref.shape[2] : (j + 1) * x_ref.shape[2]]
            btrem_ref[k + j] = bt[k + j, :, nodes:]
            bext_ref[k + j] = jnp.transpose(bt[k + j])
    inv_in.wait()
    lines_ref[...] = jnp.zeros(lines_ref.shape, F32)
    for w in range(waves):
        for t in range(share):
            square[...] = inv_ref[t, w].astype(F32)
            for c in range(per_group):
                lines_ref[w * share + t, :, c * width : (c + 1) * width] = square[
                    pl.ds(c, width // per_group, stride=per_group), :
                ]
    sent = [
        copy(ccat.at[:, pl.ds(nodes, ext - nodes)], crem_hbm, sems.at[1]),
        copy(y_ref, y_hbm, sems.at[2]),
        copy(bext_ref, bext_hbm, sems.at[3]),
    ]
    for w in range(waves):
        r_ref[w] = sum(dot(bt[k, :, :nodes], x_ref[k]) for k in (2 * w, 2 * w + 1))
    for moved in sent:
        moved.wait()


def prepare(slots, basis_t, coarse_inv, x4, ext, per_group, share):
    parts, nodes, width = x4.shape
    patches, patch_nodes = slots.shape
    rest = patch_nodes - nodes // patches
    columns = patches * basis_t.shape[2]
    y = ((parts, patches * rest, width), BF16)
    b_ext = ((parts, ext, columns), BF16)
    size = coarse_inv.shape[3]
    waves = coarse_inv.shape[1]
    assert coarse_inv.shape[0] % share == 0
    return call(
        functools.partial(prep_kernel, per_group, share),
        16,
        [lax.axis_index("patch").astype(jnp.int32).reshape(1)],
        [basis_t, coarse_inv],
        [slots, x4],
        [((patches * rest, ext - nodes), BF16), y, b_ext],
        [
            ((patches, patch_nodes), F32),
            ((8, patches * rest), F32),
            ((parts // 2, columns, width), F32),
            ((parts, columns, ext - nodes), BF16),
            ((waves * share, size // per_group, LANES), F32),
        ],
        [
            vmem((patches * rest, ext), BF16),
            vmem((parts, columns, ext), BF16),
            vmem(basis_t.shape, BF16),
            vmem(*y),
            vmem(*b_ext),
            vmem((patches, patch_nodes, patch_nodes), BF16),
            vmem((share,) + coarse_inv.shape[1:], BF16),
            vmem((size, size), F32),
            pltpu.SemaphoreType.DMA((5,)),
        ],
    )


def owner_order(columns, patches, width, per_group):
    rows = patches * per_group
    i = iota((columns, columns), 0)
    j = iota((columns, columns), 1)
    source = ((i % rows) // per_group) * width + (i // rows) * per_group + i % per_group
    return (source == j).astype(F32).astype(BF16)


def restrict_kernel(
    per_group, block_ref, r_ref, btrem_ref, below_ref, above_ref, lines_ref,
    far_hbm, out_hbm, out_ref, sems,
):
    waves, columns, width = r_ref.shape
    patches = block_ref.shape[0]
    slots = below_ref.shape[1]
    rows = patches * per_group
    groups = columns // rows
    halves = width // LANES
    sent = [
        copy(below_ref, far_hbm.at[:, pl.ds(0, slots)], sems.at[0]),
        copy(above_ref, far_hbm.at[:, pl.ds(slots, slots)], sems.at[1]),
    ]
    order = owner_order(columns, patches, columns // patches, per_group)
    tail = out_ref.shape[1] - rows
    keys = jnp.zeros((tail, LANES), F32)
    for p in range(patches):
        keys = jnp.where(iota((tail, LANES), 0) == p, block_ref[p].astype(F32), keys)
    share = lines_ref.shape[0] // waves
    for w in range(waves):
        total = r_ref[w]
        for q in range(2):
            k = 2 * w + q
            total = total + dot(btrem_ref[k, :, :slots], below_ref[k])
            total = total + dot(btrem_ref[k, :, slots:], above_ref[k])
        moved = dot(order, total.astype(BF16)).astype(BF16)
        for g in range(groups):
            last = keys
            for t in range(share):
                line = jnp.broadcast_to(lines_ref[w * share + t, g : g + 1, :], keys.shape)
                last = jnp.where(iota((tail, LANES), 0) == patches + t, line, last)
            last = last.astype(BF16)
            for h in range(halves):
                owner = (w * groups + g) * halves + h
                out_ref[owner, :rows, :] = moved[g * rows : (g + 1) * rows, h * LANES : (h + 1) * LANES]
                out_ref[owner, rows:, :] = last
        part = pl.ds(w * groups * halves, groups * halves)
        sent.append(copy(out_ref.at[part], out_hbm.at[part], sems.at[2 + w], 1))
    for copied in sent:
        copied.wait()


def restrict(block, r_own, bt_rem, below, above, lines, owners, per_group, padded):
    parts, slots, width = below.shape
    out = ((owners, padded, LANES), BF16)
    return call(
        functools.partial(restrict_kernel, per_group),
        3,
        [block],
        [],
        [r_own, bt_rem, below, above, lines],
        [((parts, 2 * slots, width), BF16), out],
        [],
        [vmem(*out), pltpu.SemaphoreType.DMA((2 + r_own.shape[0],))],
    )


def sums_kernel(per_group, patches, coarse_count, blocks, share, got_ref, out_ref, data, tags):
    owners, padded, _ = got_ref.shape
    rows = patches * per_group
    tail = padded - rows
    for s in range(owners):
        data[s * rows : (s + 1) * rows, :] = got_ref[s, :rows, :].astype(F32)
        tags[s * tail : (s + 1) * tail, :] = got_ref[s, rows:, :].astype(F32)
    tag = tags[...].astype(BF16)
    count = owners * rows
    i = iota((count, owners * tail), 0)
    j = iota((count, owners * tail), 1)
    wanted = (i // rows) * tail + (i % rows) // per_group
    keys = dot((wanted == j).astype(F32).astype(BF16), tag)
    keys = keys * float(per_group) + (iota((count, LANES), 0) % per_group).astype(F32)
    key_row = jnp.transpose(keys)[0:1, :]
    column = jnp.concatenate([keys] * (count // LANES), axis=1)
    same = (column == key_row).astype(F32).astype(BF16)
    data[...] = dot(same, data[...].astype(BF16))

    pairs = owners * patches
    i = iota((pairs, owners * tail), 0)
    j = iota((pairs, owners * tail), 1)
    named = dot(((i // patches) * tail + i % patches == j).astype(F32).astype(BF16), tag)
    source, place = j // tail, j % tail - patches
    block = (source // coarse_count) * share + place
    held = (place >= 0) & (place < share) & (block < blocks)
    block = jnp.where(held, (source % coarse_count) * blocks + block, -1).astype(F32)
    if owners * tail >= LANES:
        named = jnp.concatenate([named] * (owners * tail // LANES), axis=1)
    tags[0:pairs, :] = dot((named == block).astype(F32).astype(BF16), tag)
    extra = out_ref.shape[1] - rows - patches
    for s in range(owners):
        out_ref[s, :rows, :] = data[s * rows : (s + 1) * rows, :].astype(BF16)
        last = tags[s * patches : (s + 1) * patches, :]
        if extra:
            last = jnp.concatenate([last, jnp.zeros((extra, LANES), F32)], axis=0)
        out_ref[s, rows:, :] = last.astype(BF16)


def owner_sums(got, patches, per_group, blocks, share):
    owners, padded, _ = got.shape
    rows = patches * per_group
    back = -(-(rows + patches) // 8) * 8
    out = ((owners, back, LANES), BF16)
    return call(
        functools.partial(
            sums_kernel, per_group, patches, lax.axis_size("coarse"), blocks, share
        ),
        6,
        [],
        [],
        [got],
        [],
        [out],
        [
            vmem((owners * rows, LANES), F32),
            vmem((owners * (padded - rows), LANES), F32),
        ],
    )[0]


def local_kernel(
    first, inv_hbm, x_hbm, y_hbm, crem_hbm, far_hbm, pos_ref,
    local_hbm, rest_hbm,
    g, inv_ref, x_ref, y_ref, crem_ref, far_ref, local_ref, rest_ref, order_ref, back_ref,
    sems, inv_sems, out_sems,
):
    parts, rows, width = x_ref.shape
    count, waves = inv_ref.shape[:2]
    patch_nodes = pos_ref.shape[1]
    core = rows // count
    rest = patch_nodes - core
    mine = pl.ds(first * rest, count * rest)
    small = [
        copy(crem_hbm.at[mine], crem_ref, sems.at[0]),
        copy(far_hbm, far_ref, sems.at[1]),
        copy(y_hbm.at[:, mine], y_ref, sems.at[2]),
        copy(x_hbm.at[:, pl.ds(first * core, rows)], x_ref, sems.at[3]),
    ]
    inverses = {
        (i, w): copy(inv_hbm.at[first + i, w], inv_ref.at[i, w], inv_sems.at[i * waves + w], 1)
        for i in range(count)
        for w in range(waves)
    }
    for i in range(count):
        prow = pos_ref[first + i : first + i + 1, :]
        order_ref[i] = one_hot_rows(as_column(prow), patch_nodes)
        places = (iota((rest, patch_nodes), 0) + core).astype(F32)
        back_ref[i] = (prow == places).astype(F32).astype(BF16)
    for moved in small:
        moved.wait()
    for i in range(count):
        here = slice(i * rest, (i + 1) * rest)
        for k in range(0, parts, 2):
            far = dot(crem_ref[here, :], beside([far_ref[k], far_ref[k + 1]]))
            other = beside([y_ref[k, here, :], y_ref[k + 1, here, :]]) + far.astype(BF16)
            rows = slice(i * core, (i + 1) * core)
            mine = beside([x_ref[k, rows, :], x_ref[k + 1, rows, :]])
            moved = dot(order_ref[i], jnp.concatenate([mine, other], axis=0)).astype(BF16)
            for j in range(2):
                at = (k + j) * patch_nodes
                g[i, at : at + patch_nodes, :] = moved[:, j * width : (j + 1) * width]
    sent = []
    for i in range(count):
        here = slice(i * rest, (i + 1) * rest)
        for w in range(waves):
            inverses[i, w].wait()
        for w in range(waves):
            terms = g[i, 2 * w * patch_nodes : 2 * (w + 1) * patch_nodes, :]
            local_ref[i, w] = dot_in_halves(inv_ref.at[i, w], terms).astype(BF16)
        sent.append(copy(local_ref.at[i], local_hbm.at[i], out_sems.at[i]))
        for w in range(waves):
            pair = beside([local_ref[i, w, :patch_nodes, :], local_ref[i, w, patch_nodes:, :]])
            got = dot(back_ref[i], pair).astype(BF16)
            for j in range(2):
                rest_ref[2 * w + j, here, :] = got[:, j * width : (j + 1) * width]
    sent.append(copy(rest_ref, rest_hbm, sems.at[0]))
    for moved in sent:
        moved.wait()


def local_products(pos, x4, y, crem, far, patch_inv, first, count):
    parts, nodes, width = x4.shape
    patches, patch_nodes = pos.shape
    core = nodes // patches
    rest = patch_nodes - core
    waves = patch_inv.shape[1]
    local = ((count, waves, 2 * patch_nodes, width), BF16)
    others = ((parts, count * rest, width), BF16)
    return call(
        functools.partial(local_kernel, first),
        24,
        [],
        [patch_inv, x4, y, crem, far],
        [pos],
        [local, others],
        [],
        [
            vmem((count, parts * patch_nodes, width), BF16),
            vmem((count,) + patch_inv.shape[1:], BF16),
            vmem((parts, count * core, width), BF16),
            vmem(*others),
            vmem((count * rest, crem.shape[1]), BF16),
            vmem((parts, crem.shape[1], width), BF16),
            vmem(*local),
            vmem(*others),
            vmem((count, patch_nodes, patch_nodes), BF16),
            vmem((count, rest, patch_nodes), BF16),
            pltpu.SemaphoreType.DMA((4,)),
            pltpu.SemaphoreType.DMA((count * waves,)),
            pltpu.SemaphoreType.DMA((count,)),
        ],
    )


def coef_kernel(
    per_group, patches, bext_hbm, *refs
):
    *other_hbm, sums_ref, rest_ref, coef_ref, low_ref, high_ref = refs[:-5]
    gathered, inverses, brem_ref, other_ref, sems = refs[-5:]
    slots = low_ref.shape[1]
    nodes = bext_hbm.shape[1] - 2 * slots
    arriving = [copy(bext_hbm.at[:, pl.ds(nodes, 2 * slots)], brem_ref, sems.at[0])]
    start = 0
    for i, other in enumerate(other_hbm):
        place = pl.ds(start, other.shape[1])
        arriving.append(copy(other, other_ref.at[:, place], sems.at[1 + i]))
        start += other.shape[1]
    waves, columns, width = coef_ref.shape
    size = columns // patches
    rows = patches * per_group
    groups = columns // rows
    halves = width // LANES
    held = groups * patches
    i = iota((columns, held), 0)
    j = iota((columns, held), 1)
    grow = ((i % size) // per_group * patches + i // size == j).astype(F32).astype(BF16)
    in_lanes = iota((columns, LANES), 1) // size == iota((columns, LANES), 0) % per_group
    i = iota((LANES, columns), 0)
    j = iota((LANES, columns), 1)
    fold = (i % size == (j // rows) * per_group + j % per_group).astype(F32).astype(BF16)
    i = iota((columns, columns), 0)
    j = iota((columns, columns), 1)
    in_patch = (j % rows) // per_group == i // size
    ids = rest_ref[0:1, :]
    reach = (2 * slots, ids.shape[1])
    spread = (ids == (iota(reach, 0) + nodes).astype(F32)).astype(F32).astype(BF16)
    for w in range(waves):
        for g in range(groups):
            for h in range(halves):
                owner = (w * groups + g) * halves + h
                gathered[g * rows : (g + 1) * rows, h * LANES : (h + 1) * LANES] = sums_ref[
                    owner, :rows, :
                ].astype(F32)
            inverses[g * patches : (g + 1) * patches, :] = sums_ref[
                (w * groups + g) * halves, rows : rows + patches, :
            ].astype(F32)
        grown = dot(grow, inverses[...].astype(BF16))
        folded = dot(jnp.where(in_lanes, grown, 0.0).astype(BF16), fold)
        inverse = jnp.where(in_patch, folded, 0.0).astype(BF16)
        coef = dot(inverse, gathered[...].astype(BF16)).astype(BF16)
        coef_ref[w] = coef
        if w == 0:
            for moved in arriving:
                moved.wait()
        for q in range(2):
            k = 2 * w + q
            margin = (dot(spread, other_ref[k]) + dot(brem_ref[k], coef)).astype(BF16)
            low_ref[k] = margin[:slots]
            high_ref[k] = margin[slots:]


def coefficients(sums, b_ext, rest_ids, others, patches, slots, per_group):
    parts, _, columns = b_ext.shape
    width = others[0].shape[2]
    groups = columns // (patches * per_group)
    margin = ((parts, slots, width), BF16)
    return call(
        functools.partial(coef_kernel, per_group, patches),
        6,
        [],
        [b_ext] + others,
        [sums, rest_ids],
        [],
        [((parts // 2, columns, width), BF16), margin, margin],
        [
            vmem((columns, width), F32),
            vmem((groups * patches, LANES), F32),
            vmem((parts, 2 * slots, columns), BF16),
            vmem((parts, rest_ids.shape[1], width), BF16),
            pltpu.SemaphoreType.DMA((1 + len(others),)),
        ],
    )


def own_kernel(bext_hbm, *refs):
    *pairs, rows_ref, rest_ref, pos_ref, coef_ref, out_ref, back_ref, bown_ref, local_ref, other_ref, sems = refs
    half = len(pairs) // 2
    parts, nodes, _ = out_ref.shape
    patches, patch_nodes = pos_ref.shape
    core = nodes // patches
    arriving = []
    for k in range(parts):
        moves = [(bext_hbm.at[k, pl.ds(0, nodes)], bown_ref.at[k])]
        start = 0
        for a in pairs[half:]:
            moves.append((a.at[k], other_ref.at[k, pl.ds(start, a.shape[1])]))
            start += a.shape[1]
        start = 0
        terms = pl.ds((k % 2) * patch_nodes, patch_nodes)
        for a in pairs[:half]:
            here = pl.ds(start, a.shape[0])
            moves.append((a.at[:, k // 2, terms], local_ref.at[k, here], 1))
            start += a.shape[0]
        arriving.append([copy(m[0], m[1], sems.at[k, i], *m[2:]) for i, m in enumerate(moves)])
    slots = rows_ref.shape[1]
    for b in range(2):
        ids = rows_ref[b : b + 1, :].astype(F32)
        back_ref[:, b * slots : (b + 1) * slots] = (
            (ids == iota((nodes, slots), 0).astype(F32)).astype(F32).astype(BF16)
        )
    ids = rest_ref[0:1, :]
    shape = (nodes, ids.shape[1])
    spread = (ids == iota(shape, 0).astype(F32)).astype(F32).astype(BF16)
    places = iota((core, patch_nodes), 0).astype(F32)
    backs = [
        (pos_ref[p : p + 1, :] == places).astype(F32).astype(BF16) for p in range(patches)
    ]
    width = out_ref.shape[2]
    for k in range(0, parts, 2):
        for moved in arriving[k] + arriving[k + 1]:
            moved.wait()
        total = dot(spread, beside([other_ref[k], other_ref[k + 1]]))
        cores = [
            dot(backs[p], beside([local_ref[k, p], local_ref[k + 1, p]])) for p in range(patches)
        ]
        total = total + jnp.concatenate(cores, axis=0)
        for j in range(2):
            coarse = dot(bown_ref[k + j], coef_ref[(k + j) // 2])
            out_ref[k + j] = total[:, j * width : (j + 1) * width] + coarse


def own_rows(b_ext, coef, rows, rest_ids, pos, locals_, others, nodes):
    parts, _, columns = b_ext.shape
    width = coef.shape[2]
    return call(
        own_kernel,
        20,
        [],
        [b_ext] + locals_ + others,
        [rows, rest_ids, pos, coef],
        [],
        [((parts, nodes, width), F32), ((nodes, 2 * rows.shape[1]), BF16)],
        [
            vmem((parts, nodes, columns), BF16),
            vmem((parts,) + pos.shape + (width,), BF16),
            vmem((parts, rest_ids.shape[1], width), BF16),
            pltpu.SemaphoreType.DMA((parts, 1 + len(locals_) + len(others))),
        ],
    )


def final_kernel(own_ref, spread_ref, above_ref, below_ref, out_hbm, out_ref, sems):
    parts, _, width = own_ref.shape
    sent = []
    for k in range(0, parts, 2):
        back = jnp.concatenate(
            [beside([a[k], a[k + 1]]) for a in (above_ref, below_ref)], axis=0
        )
        total = dot(spread_ref[...], back)
        for j in range(2):
            mine = total[:, j * width : (j + 1) * width]
            out_ref[k + j] = (own_ref[k + j] + mine).astype(BF16)
            sent.append(copy(out_ref.at[k + j], out_hbm.at[k + j], sems.at[k + j]))
    for moved in sent:
        moved.wait()


def finish(own, spread, above, below):
    return call(
        final_kernel,
        12,
        [],
        [],
        [own, spread, above, below],
        [(own.shape, BF16)],
        [],
        [vmem(own.shape, BF16), pltpu.SemaphoreType.DMA((own.shape[0],))],
    )[0]


def per_device(residual, patch_inv, coarse_basis, coarse_inv, patch_slots, send_rows, coarse_block):
    waves, _, nodes, width = residual.shape
    patches = patch_inv.shape[0]
    size = coarse_basis.shape[3]
    slots = send_rows.shape[2]
    ext = nodes + 2 * slots
    owners = lax.axis_size(AXES)
    halves = width // LANES
    groups = owners // (waves * halves)
    per_group = size // groups
    assert groups * waves * halves == owners and per_group * groups == size
    blocks = coarse_inv.shape[0]
    share = -(-blocks // lax.axis_size("patch"))
    rows = patches * per_group
    padded = -(-(rows + patches + share) // 8) * 8
    half = patches // 2
    send = send_rows[0]
    basis_t = jnp.swapaxes(coarse_basis, 2, 3)

    x_all = residual.reshape(2 * waves, nodes, width)
    up, down, x4, slots_v = select_rows(x_all, send, patch_slots)
    below = passed_along(up, AXES, 1)
    above = passed_along(down, AXES, -1)
    crem, y, b_ext, pos, rest_ids, r_own, bt_rem, lines = prepare(
        slots_v, basis_t, coarse_inv, x4, ext, per_group, share
    )
    far, sent = restrict(
        coarse_block, r_own, bt_rem, below, above, lines, owners, per_group, padded
    )
    got = lax.all_to_all(sent, AXES, 0, 0, tiled=True)
    local_a, rest_a = local_products(pos, x_all, y, crem, far, patch_inv, 0, half)
    sums = owner_sums(got, patches, per_group, blocks, share)
    mine = lax.all_to_all(sums, AXES, 0, 0, tiled=True)
    local_b, rest_b = local_products(pos, x_all, y, crem, far, patch_inv, half, patches - half)
    coef, low, high = coefficients(
        mine, b_ext, rest_ids, [rest_a, rest_b], patches, slots, per_group
    )
    back_above = passed_along(low, AXES, -1)
    back_below = passed_along(high, AXES, 1)
    own, spread = own_rows(b_ext, coef, send, rest_ids, pos, [local_a, local_b], [rest_a, rest_b], nodes)
    out = finish(own, spread, back_above, back_below)
    return out.reshape(residual.shape)


def solution(mesh):
    placed = (
        P(None, None, AXES, None),
        P(AXES, None, None, None),
        P(AXES, None, None, None),
        P("coarse", None, None, None),
        P(AXES, None),
        P(AXES, None, None),
        P(AXES),
    )
    return jax.shard_map(
        per_device,
        mesh=mesh,
        in_specs=placed,
        out_specs=P(None, None, AXES, None),
        check_vma=False,
    )
```

```python
import functools

import jax
import jax.numpy as jnp
from jax import lax
from jax.experimental import pallas as pl
from jax.experimental.pallas import tpu as pltpu
from jax.sharding import PartitionSpec as P


AXES = ("patch", "coarse")
LANES = 128
MIB = 1 << 20
F32 = jnp.float32
BF16 = jnp.bfloat16


def swapped(value, axis, odd_first):
    count = lax.axis_size(axis)
    shift = int(odd_first)
    partner = {(i + shift) % count: ((i ^ 1) + shift) % count for i in range(count)}
    return lax.ppermute(value, axis, sorted(partner.items()))


def dot(a, b):
    return jnp.dot(a, b, preferred_element_type=F32)


def beside(parts):
    return jnp.concatenate(parts, axis=1)


def dot_in_halves(a_ref, b):
    half = b.shape[0] // 2
    return dot(a_ref[:, :half], b[:half]) + dot(a_ref[:, half:], b[half:])


def as_column(row):
    return jnp.transpose(jnp.broadcast_to(row, (LANES, row.shape[1])))


def iota(shape, axis):
    return lax.broadcasted_iota(jnp.int32, shape, axis)


def one_hot_rows(column, width, start=0):
    rows = column.shape[0]
    parts = [
        (column == (iota((rows, LANES), 1) + (start + t)).astype(F32)).astype(F32).astype(BF16)
        for t in range(0, width, LANES)
    ]
    return jnp.concatenate(parts, axis=1)


def vmem(shape, dtype):
    return pltpu.VMEM(shape, dtype)


def resident(array):
    return pltpu.with_memory_space_constraint(array, pltpu.VMEM)


def call(kernel, limit, smem, far, near, far_out, near_out, scratch=()):
    spaces = [pltpu.SMEM] * len(smem) + [pltpu.HBM] * len(far) + [pltpu.VMEM] * len(near)
    out_spaces = [pltpu.HBM] * len(far_out) + [pltpu.VMEM] * len(near_out)
    return pl.pallas_call(
        kernel,
        in_specs=[pl.BlockSpec(memory_space=m) for m in spaces],
        out_specs=[pl.BlockSpec(memory_space=m) for m in out_spaces],
        out_shape=[pltpu.HBM(*o) for o in far_out] + [vmem(*o) for o in near_out],
        scratch_shapes=list(scratch),
        compiler_params=pltpu.CompilerParams(vmem_limit_bytes=limit * MIB),
    )(
        *smem,
        *[pltpu.with_memory_space_constraint(a, pltpu.HBM) for a in far],
        *[resident(a) for a in near],
    )


def copy(source, target, sem, priority=0):
    moved = pltpu.make_async_copy(source, target, sem)
    moved.start(priority=priority)
    return moved


def partner_rows(rows_ref, odd):
    up, down = (rows_ref[b : b + 1, :].astype(F32) for b in range(2))
    return jnp.where(odd == 0, up, down), jnp.where(odd == 0, down, up)


def select_kernel(
    odd_ref, x_hbm, rows_hbm, slots_hbm, near_ref, far_ref, slots_ref,
    x_ref, rows_ref, arrived,
):
    slots = rows_ref.shape[1]
    parts, nodes, _ = x_ref.shape
    small = pltpu.make_async_copy(rows_hbm, rows_ref, arrived.at[parts])
    copies = [pltpu.make_async_copy(x_hbm.at[k], x_ref.at[k], arrived.at[k]) for k in range(parts)]
    later = pltpu.make_async_copy(slots_hbm, slots_ref, arrived.at[parts + 1])
    for copy in [small] + copies + [later]:
        copy.start()
    small.wait()
    pick = jnp.concatenate(
        [one_hot_rows(as_column(ids), nodes) for ids in partner_rows(rows_ref, odd_ref[0])], axis=0
    )
    width = x_ref.shape[2]
    for k in range(0, parts, 2):
        copies[k].wait()
        copies[k + 1].wait()
        got = dot(pick, beside([x_ref[k], x_ref[k + 1]])).astype(BF16)
        for j in range(2):
            near_ref[k + j] = got[:slots, j * width : (j + 1) * width]
            far_ref[k + j] = got[slots:, j * width : (j + 1) * width]
    later.wait()


def select_rows(x4, rows, patch_slots, odd):
    parts, _, width = x4.shape
    margin = ((parts, rows.shape[1], width), BF16)
    return call(
        select_kernel,
        10,
        [odd],
        [x4, rows, patch_slots],
        [],
        [],
        [margin, margin, (patch_slots.shape, patch_slots.dtype)],
        [vmem(x4.shape, BF16), vmem(rows.shape, rows.dtype), pltpu.SemaphoreType.DMA((parts + 2,))],
    )


def prep_kernel(
    per_group, share, place_ref, basis_hbm, inv_hbm, x_hbm, slots_ref,
    crem_hbm, y_hbm, bext_hbm, pos_ref, rest_ref, r_ref, btrem_ref, lines_ref,
    ccat, bt, basis_ref, y_ref, bext_ref, order_ref, inv_ref, square, x_ref, sems,
):
    basis_in = copy(basis_hbm, basis_ref, sems.at[0])
    held = jnp.minimum(place_ref[0] * share, inv_hbm.shape[0] - share)
    inv_in = copy(inv_hbm.at[pl.ds(held, share)], inv_ref, sems.at[4])
    x_in = copy(x_hbm, x_ref, sems.at[5], 1)
    patches, patch_nodes = slots_ref.shape
    waves, width = basis_ref.shape[1], basis_ref.shape[2]
    parts, nodes, _ = x_ref.shape
    core = nodes // patches
    rest = patch_nodes - core
    ext = ccat.shape[1]
    slots = slots_ref[...].astype(F32)
    first = (iota((patches, patch_nodes), 0) * core).astype(F32)
    local = slots - first
    outside = (local < 0.0) | (local >= float(core))
    before = iota((patch_nodes, patch_nodes), 0) < iota((patch_nodes, patch_nodes), 1)
    rank = dot(outside.astype(F32).astype(BF16), before.astype(F32).astype(BF16))
    pos = jnp.where(outside, rank + float(core), local)
    pos_ref[...] = pos
    for p in range(patches):
        prow = pos[p : p + 1, :]
        order_ref[p] = one_hot_rows(as_column(prow), patch_nodes)
        hit = prow == (iota((rest, patch_nodes), 0) + core).astype(F32)
        ids = jnp.sum(
            jnp.where(hit, jnp.broadcast_to(slots[p : p + 1, :], hit.shape), 0.0),
            axis=1,
            keepdims=True,
        )
        ids = jnp.broadcast_to(ids, (rest, LANES))
        rest_ref[:, p * rest : (p + 1) * rest] = jnp.transpose(ids)[0:8]
        ccat[p * rest : (p + 1) * rest, :] = one_hot_rows(ids, ext)
    basis_in.wait()
    for p in range(patches):
        basis = jnp.concatenate(
            [
                basis_ref[p, w, :, q * patch_nodes : (q + 1) * patch_nodes]
                for w in range(waves)
                for q in range(2)
            ],
            axis=0,
        )
        moved = dot(basis, order_ref[p]).astype(BF16)
        spread = dot(moved[:, core:], ccat[p * rest : (p + 1) * rest, :]).astype(BF16)
        for k in range(parts):
            rows = slice(k * width, (k + 1) * width)
            here = slice(p * width, (p + 1) * width)
            bt[k, here, :] = spread[rows]
            bt[k, here, p * core : (p + 1) * core] = (
                spread[rows, p * core : (p + 1) * core] + moved[rows, :core]
            )
    x_in.wait()
    for k in range(0, parts, 2):
        both = dot(ccat[:, :nodes], beside([x_ref[k], x_ref[k + 1]])).astype(BF16)
        for j in range(2):
            y_ref[k + j] = both[:, j * x_ref.shape[2] : (j + 1) * x_ref.shape[2]]
            btrem_ref[k + j] = bt[k + j, :, nodes:]
            bext_ref[k + j] = jnp.transpose(bt[k + j])
    inv_in.wait()
    lines_ref[...] = jnp.zeros(lines_ref.shape, F32)
    for w in range(waves):
        for t in range(share):
            square[...] = inv_ref[t, w].astype(F32)
            for c in range(per_group):
                lines_ref[w * share + t, :, c * width : (c + 1) * width] = square[
                    pl.ds(c, width // per_group, stride=per_group), :
                ]
    sent = [
        copy(ccat.at[:, pl.ds(nodes, ext - nodes)], crem_hbm, sems.at[1]),
        copy(y_ref, y_hbm, sems.at[2]),
        copy(bext_ref, bext_hbm, sems.at[3]),
    ]
    for w in range(waves):
        r_ref[w] = sum(dot(bt[k, :, :nodes], x_ref[k]) for k in (2 * w, 2 * w + 1))
    for moved in sent:
        moved.wait()


def prepare(slots, basis_t, coarse_inv, x4, ext, per_group, share):
    parts, nodes, width = x4.shape
    patches, patch_nodes = slots.shape
    rest = patch_nodes - nodes // patches
    columns = patches * basis_t.shape[2]
    y = ((parts, patches * rest, width), BF16)
    b_ext = ((parts, ext, columns), BF16)
    size = coarse_inv.shape[3]
    waves = coarse_inv.shape[1]
    assert coarse_inv.shape[0] % share == 0
    return call(
        functools.partial(prep_kernel, per_group, share),
        20,
        [lax.axis_index("patch").astype(jnp.int32).reshape(1)],
        [basis_t, coarse_inv, x4],
        [slots],
        [((patches * rest, ext - nodes), BF16), y, b_ext],
        [
            ((patches, patch_nodes), F32),
            ((8, patches * rest), F32),
            ((parts // 2, columns, width), F32),
            ((parts, columns, ext - nodes), BF16),
            ((waves * share, size // per_group, LANES), F32),
        ],
        [
            vmem((patches * rest, ext), BF16),
            vmem((parts, columns, ext), BF16),
            vmem(basis_t.shape, BF16),
            vmem(*y),
            vmem(*b_ext),
            vmem((patches, patch_nodes, patch_nodes), BF16),
            vmem((share,) + coarse_inv.shape[1:], BF16),
            vmem((size, size), F32),
            vmem(x4.shape, BF16),
            pltpu.SemaphoreType.DMA((6,)),
        ],
    )


def owner_order(columns, patches, width, per_group):
    rows = patches * per_group
    i = iota((columns, columns), 0)
    j = iota((columns, columns), 1)
    source = ((i % rows) // per_group) * width + (i // rows) * per_group + i % per_group
    return (source == j).astype(F32).astype(BF16)


def restrict_kernel(
    per_group, block_ref, odd_ref, r_ref, btrem_ref, near_ref, other_ref, lines_ref,
    far_hbm, out_hbm, out_ref, sems,
):
    waves, columns, width = r_ref.shape
    patches = block_ref.shape[0]
    slots = near_ref.shape[1]
    rows = patches * per_group
    groups = columns // rows
    halves = width // LANES
    odd = odd_ref[0]
    sent = [
        copy(near_ref, far_hbm.at[:, pl.ds(pl.multiple_of((1 - odd) * slots, slots), slots)], sems.at[0]),
        copy(other_ref, far_hbm.at[:, pl.ds(pl.multiple_of(odd * slots, slots), slots)], sems.at[1]),
    ]
    order = owner_order(columns, patches, columns // patches, per_group)
    tail = out_ref.shape[1] - rows
    keys = jnp.zeros((tail, LANES), F32)
    for p in range(patches):
        keys = jnp.where(iota((tail, LANES), 0) == p, block_ref[p].astype(F32), keys)
    share = lines_ref.shape[0] // waves
    for w in range(waves):
        total = r_ref[w]
        for q in range(2):
            k = 2 * w + q
            near, other = near_ref[k], other_ref[k]
            total = total + dot(btrem_ref[k, :, :slots], jnp.where(odd == 0, other, near))
            total = total + dot(btrem_ref[k, :, slots:], jnp.where(odd == 0, near, other))
        moved = dot(order, total.astype(BF16)).astype(BF16)
        for g in range(groups):
            last = keys
            for t in range(share):
                line = jnp.broadcast_to(lines_ref[w * share + t, g : g + 1, :], keys.shape)
                last = jnp.where(iota((tail, LANES), 0) == patches + t, line, last)
            last = last.astype(BF16)
            for h in range(halves):
                owner = (w * groups + g) * halves + h
                out_ref[owner, :rows, :] = moved[g * rows : (g + 1) * rows, h * LANES : (h + 1) * LANES]
                out_ref[owner, rows:, :] = last
        part = pl.ds(w * groups * halves, groups * halves)
        sent.append(copy(out_ref.at[part], out_hbm.at[part], sems.at[2 + w], 1))
    for copied in sent:
        copied.wait()


def restrict(block, odd, r_own, bt_rem, near, other, lines, owners, per_group, padded):
    parts, slots, width = near.shape
    out = ((owners, padded, LANES), BF16)
    return call(
        functools.partial(restrict_kernel, per_group),
        3,
        [block, odd],
        [],
        [r_own, bt_rem, near, other, lines],
        [((parts, 2 * slots, width), BF16), out],
        [],
        [vmem(*out), pltpu.SemaphoreType.DMA((2 + r_own.shape[0],))],
    )


def sums_kernel(per_group, patches, coarse_count, blocks, share, got_ref, out_ref, data, tags):
    owners, padded, _ = got_ref.shape
    rows = patches * per_group
    tail = padded - rows
    for s in range(owners):
        data[s * rows : (s + 1) * rows, :] = got_ref[s, :rows, :].astype(F32)
        tags[s * tail : (s + 1) * tail, :] = got_ref[s, rows:, :].astype(F32)
    tag = tags[...].astype(BF16)
    count = owners * rows
    i = iota((count, owners * tail), 0)
    j = iota((count, owners * tail), 1)
    wanted = (i // rows) * tail + (i % rows) // per_group
    keys = dot((wanted == j).astype(F32).astype(BF16), tag)
    keys = keys * float(per_group) + (iota((count, LANES), 0) % per_group).astype(F32)
    key_row = jnp.transpose(keys)[0:1, :]
    column = jnp.concatenate([keys] * (count // LANES), axis=1)
    same = (column == key_row).astype(F32).astype(BF16)
    data[...] = dot(same, data[...].astype(BF16))

    pairs = owners * patches
    i = iota((pairs, owners * tail), 0)
    j = iota((pairs, owners * tail), 1)
    named = dot(((i // patches) * tail + i % patches == j).astype(F32).astype(BF16), tag)
    source, place = j // tail, j % tail - patches
    block = (source // coarse_count) * share + place
    held = (place >= 0) & (place < share) & (block < blocks)
    block = jnp.where(held, (source % coarse_count) * blocks + block, -1).astype(F32)
    if owners * tail >= LANES:
        named = jnp.concatenate([named] * (owners * tail // LANES), axis=1)
    tags[0:pairs, :] = dot((named == block).astype(F32).astype(BF16), tag)
    extra = out_ref.shape[1] - rows - patches
    for s in range(owners):
        out_ref[s, :rows, :] = data[s * rows : (s + 1) * rows, :].astype(BF16)
        last = tags[s * patches : (s + 1) * patches, :]
        if extra:
            last = jnp.concatenate([last, jnp.zeros((extra, LANES), F32)], axis=0)
        out_ref[s, rows:, :] = last.astype(BF16)


def owner_sums(got, patches, per_group, blocks, share):
    owners, padded, _ = got.shape
    rows = patches * per_group
    back = -(-(rows + patches) // 8) * 8
    out = ((owners, back, LANES), BF16)
    return call(
        functools.partial(
            sums_kernel, per_group, patches, lax.axis_size("coarse"), blocks, share
        ),
        6,
        [],
        [],
        [got],
        [],
        [out],
        [
            vmem((owners * rows, LANES), F32),
            vmem((owners * (padded - rows), LANES), F32),
        ],
    )[0]


def local_kernel(
    first, inv_hbm, x_hbm, y_hbm, crem_hbm, far_hbm, pos_ref,
    local_hbm, rest_hbm,
    g, inv_ref, x_ref, y_ref, crem_ref, far_ref, local_ref, rest_ref, order_ref, back_ref,
    sems, inv_sems, out_sems,
):
    parts, rows, width = x_ref.shape
    count, waves = inv_ref.shape[:2]
    patch_nodes = pos_ref.shape[1]
    core = rows // count
    rest = patch_nodes - core
    mine = pl.ds(first * rest, count * rest)
    small = [
        copy(crem_hbm.at[mine], crem_ref, sems.at[0]),
        copy(far_hbm, far_ref, sems.at[1]),
        copy(y_hbm.at[:, mine], y_ref, sems.at[2]),
        copy(x_hbm.at[:, pl.ds(first * core, rows)], x_ref, sems.at[3]),
    ]
    inverses = {
        (i, w): copy(inv_hbm.at[first + i, w], inv_ref.at[i, w], inv_sems.at[i * waves + w], 1)
        for i in range(count)
        for w in range(waves)
    }
    for i in range(count):
        prow = pos_ref[first + i : first + i + 1, :]
        order_ref[i] = one_hot_rows(as_column(prow), patch_nodes)
        places = (iota((rest, patch_nodes), 0) + core).astype(F32)
        back_ref[i] = (prow == places).astype(F32).astype(BF16)
    for moved in small:
        moved.wait()
    for i in range(count):
        here = slice(i * rest, (i + 1) * rest)
        for k in range(0, parts, 2):
            far = dot(crem_ref[here, :], beside([far_ref[k], far_ref[k + 1]]))
            other = beside([y_ref[k, here, :], y_ref[k + 1, here, :]]) + far.astype(BF16)
            rows = slice(i * core, (i + 1) * core)
            mine = beside([x_ref[k, rows, :], x_ref[k + 1, rows, :]])
            moved = dot(order_ref[i], jnp.concatenate([mine, other], axis=0)).astype(BF16)
            for j in range(2):
                at = (k + j) * patch_nodes
                g[i, at : at + patch_nodes, :] = moved[:, j * width : (j + 1) * width]
    sent = []
    for i in range(count):
        here = slice(i * rest, (i + 1) * rest)
        for w in range(waves):
            inverses[i, w].wait()
        for w in range(waves):
            terms = g[i, 2 * w * patch_nodes : 2 * (w + 1) * patch_nodes, :]
            local_ref[i, w] = dot_in_halves(inv_ref.at[i, w], terms).astype(BF16)
        sent.append(copy(local_ref.at[i], local_hbm.at[i], out_sems.at[i]))
        for w in range(waves):
            pair = beside([local_ref[i, w, :patch_nodes, :], local_ref[i, w, patch_nodes:, :]])
            got = dot(back_ref[i], pair).astype(BF16)
            for j in range(2):
                rest_ref[2 * w + j, here, :] = got[:, j * width : (j + 1) * width]
    sent.append(copy(rest_ref, rest_hbm, sems.at[0]))
    for moved in sent:
        moved.wait()


def local_products(pos, x4, y, crem, far, patch_inv, first, count):
    parts, nodes, width = x4.shape
    patches, patch_nodes = pos.shape
    core = nodes // patches
    rest = patch_nodes - core
    waves = patch_inv.shape[1]
    local = ((count, waves, 2 * patch_nodes, width), BF16)
    others = ((parts, count * rest, width), BF16)
    return call(
        functools.partial(local_kernel, first),
        24,
        [],
        [patch_inv, x4, y, crem, far],
        [pos],
        [local, others],
        [],
        [
            vmem((count, parts * patch_nodes, width), BF16),
            vmem((count,) + patch_inv.shape[1:], BF16),
            vmem((parts, count * core, width), BF16),
            vmem(*others),
            vmem((count * rest, crem.shape[1]), BF16),
            vmem((parts, crem.shape[1], width), BF16),
            vmem(*local),
            vmem(*others),
            vmem((count, patch_nodes, patch_nodes), BF16),
            vmem((count, rest, patch_nodes), BF16),
            pltpu.SemaphoreType.DMA((4,)),
            pltpu.SemaphoreType.DMA((count * waves,)),
            pltpu.SemaphoreType.DMA((count,)),
        ],
    )


def coef_kernel(
    per_group, patches, odd_ref, bext_hbm, *refs
):
    *other_hbm, sums_ref, rest_ref, coef_ref, near_ref, far_ref = refs[:-5]
    gathered, inverses, brem_ref, other_ref, sems = refs[-5:]
    slots = near_ref.shape[1]
    nodes = bext_hbm.shape[1] - 2 * slots
    odd = odd_ref[0]
    starts = [pl.multiple_of(nodes + h * slots, slots) for h in (1 - odd, odd)]
    arriving = [
        copy(
            bext_hbm.at[:, pl.ds(start, slots)],
            brem_ref.at[:, pl.ds(h * slots, slots)],
            sems.at[h],
        )
        for h, start in enumerate(starts)
    ]
    start = 0
    for i, other in enumerate(other_hbm):
        place = pl.ds(start, other.shape[1])
        arriving.append(copy(other, other_ref.at[:, place], sems.at[2 + i]))
        start += other.shape[1]
    waves, columns, width = coef_ref.shape
    size = columns // patches
    rows = patches * per_group
    groups = columns // rows
    halves = width // LANES
    held = groups * patches
    i = iota((columns, held), 0)
    j = iota((columns, held), 1)
    grow = ((i % size) // per_group * patches + i // size == j).astype(F32).astype(BF16)
    in_lanes = iota((columns, LANES), 1) // size == iota((columns, LANES), 0) % per_group
    i = iota((LANES, columns), 0)
    j = iota((LANES, columns), 1)
    fold = (i % size == (j // rows) * per_group + j % per_group).astype(F32).astype(BF16)
    i = iota((columns, columns), 0)
    j = iota((columns, columns), 1)
    in_patch = (j % rows) // per_group == i // size
    ids = rest_ref[0:1, :]
    reach = (2 * slots, ids.shape[1])
    row = iota(reach, 0)
    swap = jnp.where(odd == 0, slots, 0)
    place = jnp.where(row < slots, row + swap, row - swap) + nodes
    spread = (ids == place.astype(F32)).astype(F32).astype(BF16)
    for w in range(waves):
        for g in range(groups):
            for h in range(halves):
                owner = (w * groups + g) * halves + h
                gathered[g * rows : (g + 1) * rows, h * LANES : (h + 1) * LANES] = sums_ref[
                    owner, :rows, :
                ].astype(F32)
            inverses[g * patches : (g + 1) * patches, :] = sums_ref[
                (w * groups + g) * halves, rows : rows + patches, :
            ].astype(F32)
        grown = dot(grow, inverses[...].astype(BF16))
        folded = dot(jnp.where(in_lanes, grown, 0.0).astype(BF16), fold)
        inverse = jnp.where(in_patch, folded, 0.0).astype(BF16)
        coef = dot(inverse, gathered[...].astype(BF16)).astype(BF16)
        coef_ref[w] = coef
        if w == 0:
            for moved in arriving:
                moved.wait()
        for q in range(2):
            k = 2 * w + q
            margin = (dot(spread, other_ref[k]) + dot(brem_ref[k], coef)).astype(BF16)
            near_ref[k] = margin[:slots]
            far_ref[k] = margin[slots:]


def coefficients(odd, sums, b_ext, rest_ids, others, patches, slots, per_group):
    parts, _, columns = b_ext.shape
    width = others[0].shape[2]
    groups = columns // (patches * per_group)
    margin = ((parts, slots, width), BF16)
    return call(
        functools.partial(coef_kernel, per_group, patches),
        6,
        [odd],
        [b_ext] + others,
        [sums, rest_ids],
        [],
        [((parts // 2, columns, width), BF16), margin, margin],
        [
            vmem((columns, width), F32),
            vmem((groups * patches, LANES), F32),
            vmem((parts, 2 * slots, columns), BF16),
            vmem((parts, rest_ids.shape[1], width), BF16),
            pltpu.SemaphoreType.DMA((2 + len(others),)),
        ],
    )


def own_kernel(odd_ref, bext_hbm, *refs):
    *pairs, rows_ref, rest_ref, pos_ref, coef_ref, out_ref, back_ref, bown_ref, local_ref, other_ref, sems = refs
    half = len(pairs) // 2
    parts, nodes, _ = out_ref.shape
    patches, patch_nodes = pos_ref.shape
    core = nodes // patches
    arriving = []
    for k in range(parts):
        moves = [(bext_hbm.at[k, pl.ds(0, nodes)], bown_ref.at[k])]
        start = 0
        for a in pairs[half:]:
            moves.append((a.at[k], other_ref.at[k, pl.ds(start, a.shape[1])]))
            start += a.shape[1]
        start = 0
        terms = pl.ds((k % 2) * patch_nodes, patch_nodes)
        for a in pairs[:half]:
            here = pl.ds(start, a.shape[0])
            moves.append((a.at[:, k // 2, terms], local_ref.at[k, here]))
            start += a.shape[0]
        arriving.append([copy(m[0], m[1], sems.at[k, i], int(k > 1)) for i, m in enumerate(moves)])
    slots = rows_ref.shape[1]
    for b, ids in enumerate(partner_rows(rows_ref, odd_ref[0])):
        back_ref[:, b * slots : (b + 1) * slots] = (
            (ids == iota((nodes, slots), 0).astype(F32)).astype(F32).astype(BF16)
        )
    ids = rest_ref[0:1, :]
    shape = (nodes, ids.shape[1])
    spread = (ids == iota(shape, 0).astype(F32)).astype(F32).astype(BF16)
    places = iota((core, patch_nodes), 0).astype(F32)
    backs = [
        (pos_ref[p : p + 1, :] == places).astype(F32).astype(BF16) for p in range(patches)
    ]
    width = out_ref.shape[2]
    for k in range(0, parts, 2):
        for moved in arriving[k] + arriving[k + 1]:
            moved.wait()
        total = dot(spread, beside([other_ref[k], other_ref[k + 1]]))
        cores = [
            dot(backs[p], beside([local_ref[k, p], local_ref[k + 1, p]])) for p in range(patches)
        ]
        total = total + jnp.concatenate(cores, axis=0)
        for j in range(2):
            coarse = dot(bown_ref[k + j], coef_ref[(k + j) // 2])
            out_ref[k + j] = total[:, j * width : (j + 1) * width] + coarse


def own_rows(odd, b_ext, coef, rows, rest_ids, pos, locals_, others, nodes):
    parts, _, columns = b_ext.shape
    width = coef.shape[2]
    return call(
        own_kernel,
        20,
        [odd],
        [b_ext] + locals_ + others,
        [rows, rest_ids, pos, coef],
        [],
        [((parts, nodes, width), F32), ((nodes, 2 * rows.shape[1]), BF16)],
        [
            vmem((parts, nodes, columns), BF16),
            vmem((parts,) + pos.shape + (width,), BF16),
            vmem((parts, rest_ids.shape[1], width), BF16),
            pltpu.SemaphoreType.DMA((parts, 1 + len(locals_) + len(others))),
        ],
    )


def final_kernel(own_ref, spread_ref, near_ref, other_ref, out_hbm, out_ref, sems):
    parts, _, width = own_ref.shape
    sent = []
    for k in range(0, parts, 2):
        back = jnp.concatenate(
            [beside([a[k], a[k + 1]]) for a in (near_ref, other_ref)], axis=0
        )
        total = dot(spread_ref[...], back)
        for j in range(2):
            mine = total[:, j * width : (j + 1) * width]
            out_ref[k + j] = (own_ref[k + j] + mine).astype(BF16)
            sent.append(copy(out_ref.at[k + j], out_hbm.at[k + j], sems.at[k + j]))
    for moved in sent:
        moved.wait()


def finish(own, spread, near, other):
    return call(
        final_kernel,
        12,
        [],
        [],
        [own, spread, near, other],
        [(own.shape, BF16)],
        [],
        [vmem(own.shape, BF16), pltpu.SemaphoreType.DMA((own.shape[0],))],
    )[0]


def per_device(residual, patch_inv, coarse_basis, coarse_inv, patch_slots, send_rows, coarse_block):
    waves, _, nodes, width = residual.shape
    patches = patch_inv.shape[0]
    size = coarse_basis.shape[3]
    slots = send_rows.shape[2]
    ext = nodes + 2 * slots
    owners = lax.axis_size(AXES)
    halves = width // LANES
    groups = owners // (waves * halves)
    per_group = size // groups
    assert owners % 2 == 0 and groups * waves * halves == owners and per_group * groups == size
    blocks = coarse_inv.shape[0]
    share = -(-blocks // lax.axis_size("patch"))
    rows = patches * per_group
    padded = -(-(rows + patches + share) // 8) * 8
    half = patches // 2
    send = send_rows[0]
    odd = (lax.axis_index(AXES) % 2).astype(jnp.int32).reshape(1)
    basis_t = jnp.swapaxes(coarse_basis, 2, 3)

    x_all = residual.reshape(2 * waves, nodes, width)
    to_first, to_second, slots_v = select_rows(x_all, send, patch_slots, odd)
    first_rows = swapped(to_first, AXES, False)
    second_rows = swapped(to_second, AXES, True)
    crem, y, b_ext, pos, rest_ids, r_own, bt_rem, lines = prepare(
        slots_v, basis_t, coarse_inv, x_all, ext, per_group, share
    )
    far, sent = restrict(
        coarse_block, odd, r_own, bt_rem, first_rows, second_rows, lines,
        owners, per_group, padded,
    )
    got = lax.all_to_all(sent, AXES, 0, 0, tiled=True)
    local_a, rest_a = local_products(pos, x_all, y, crem, far, patch_inv, 0, half)
    sums = owner_sums(got, patches, per_group, blocks, share)
    mine = lax.all_to_all(sums, AXES, 0, 0, tiled=True)
    local_b, rest_b = local_products(pos, x_all, y, crem, far, patch_inv, half, patches - half)
    coef, to_first, to_second = coefficients(
        odd, mine, b_ext, rest_ids, [rest_a, rest_b], patches, slots, per_group
    )
    first_back = swapped(to_first, AXES, False)
    second_back = swapped(to_second, AXES, True)
    own, spread = own_rows(odd, b_ext, coef, send, rest_ids, pos, [local_a, local_b], [rest_a, rest_b], nodes)
    out = finish(own, spread, first_back, second_back)
    return out.reshape(residual.shape)


def solution(mesh):
    placed = (
        P(None, None, AXES, None),
        P(AXES, None, None, None),
        P(AXES, None, None, None),
        P("coarse", None, None, None),
        P(AXES, None),
        P(AXES, None, None),
        P(AXES),
    )
    return jax.shard_map(
        per_device,
        mesh=mesh,
        in_specs=placed,
        out_specs=P(None, None, AXES, None),
        check_vma=False,
    )
```

```python
import functools

import jax
import jax.numpy as jnp
from jax import lax
from jax.experimental import pallas as pl
from jax.experimental.pallas import tpu as pltpu
from jax.sharding import PartitionSpec as P


AXES = ("patch", "coarse")
LANES = 128
MIB = 1 << 20
F32 = jnp.float32
BF16 = jnp.bfloat16


def swapped(value, axis, odd_first):
    count = lax.axis_size(axis)
    shift = int(odd_first)
    partner = {(i + shift) % count: ((i ^ 1) + shift) % count for i in range(count)}
    return lax.ppermute(value, axis, sorted(partner.items()))


def dot(a, b):
    return jnp.dot(a, b, preferred_element_type=F32)


def beside(parts):
    return jnp.concatenate(parts, axis=1)


def dot_in_halves(a_ref, b):
    half = b.shape[0] // 2
    return dot(a_ref[:, :half], b[:half]) + dot(a_ref[:, half:], b[half:])


def as_column(row):
    return jnp.transpose(jnp.broadcast_to(row, (LANES, row.shape[1])))


def iota(shape, axis):
    return lax.broadcasted_iota(jnp.int32, shape, axis)


def one_hot_rows(column, width, start=0):
    rows = column.shape[0]
    parts = [
        (column == (iota((rows, LANES), 1) + (start + t)).astype(F32)).astype(F32).astype(BF16)
        for t in range(0, width, LANES)
    ]
    return jnp.concatenate(parts, axis=1)


def vmem(shape, dtype):
    return pltpu.VMEM(shape, dtype)


def resident(array):
    return pltpu.with_memory_space_constraint(array, pltpu.VMEM)


def call(kernel, limit, smem, far, near, far_out, near_out, scratch=()):
    spaces = [pltpu.SMEM] * len(smem) + [pltpu.HBM] * len(far) + [pltpu.VMEM] * len(near)
    out_spaces = [pltpu.HBM] * len(far_out) + [pltpu.VMEM] * len(near_out)
    return pl.pallas_call(
        kernel,
        in_specs=[pl.BlockSpec(memory_space=m) for m in spaces],
        out_specs=[pl.BlockSpec(memory_space=m) for m in out_spaces],
        out_shape=[pltpu.HBM(*o) for o in far_out] + [vmem(*o) for o in near_out],
        scratch_shapes=list(scratch),
        compiler_params=pltpu.CompilerParams(vmem_limit_bytes=limit * MIB),
    )(
        *smem,
        *[pltpu.with_memory_space_constraint(a, pltpu.HBM) for a in far],
        *[resident(a) for a in near],
    )


def copy(source, target, sem, priority=0):
    moved = pltpu.make_async_copy(source, target, sem)
    moved.start(priority=priority)
    return moved


def partner_rows(rows_ref, odd):
    up, down = (rows_ref[b : b + 1, :].astype(F32) for b in range(2))
    return jnp.where(odd == 0, up, down), jnp.where(odd == 0, down, up)


def select_kernel(
    odd_ref, x_hbm, rows_hbm, slots_hbm, near_ref, far_ref, slots_ref,
    x_ref, rows_ref, arrived,
):
    slots = rows_ref.shape[1]
    parts, nodes, _ = x_ref.shape
    small = pltpu.make_async_copy(rows_hbm, rows_ref, arrived.at[parts])
    copies = [pltpu.make_async_copy(x_hbm.at[k], x_ref.at[k], arrived.at[k]) for k in range(parts)]
    later = pltpu.make_async_copy(slots_hbm, slots_ref, arrived.at[parts + 1])
    for copy in [small] + copies + [later]:
        copy.start()
    small.wait()
    pick = jnp.concatenate(
        [one_hot_rows(as_column(ids), nodes) for ids in partner_rows(rows_ref, odd_ref[0])], axis=0
    )
    width = x_ref.shape[2]
    for k in range(0, parts, 2):
        copies[k].wait()
        copies[k + 1].wait()
        got = dot(pick, beside([x_ref[k], x_ref[k + 1]])).astype(BF16)
        for j in range(2):
            near_ref[k + j] = got[:slots, j * width : (j + 1) * width]
            far_ref[k + j] = got[slots:, j * width : (j + 1) * width]
    later.wait()


def select_rows(x4, rows, patch_slots, odd):
    parts, _, width = x4.shape
    margin = ((parts, rows.shape[1], width), BF16)
    return call(
        select_kernel,
        10,
        [odd],
        [x4, rows, patch_slots],
        [],
        [],
        [margin, margin, (patch_slots.shape, patch_slots.dtype)],
        [vmem(x4.shape, BF16), vmem(rows.shape, rows.dtype), pltpu.SemaphoreType.DMA((parts + 2,))],
    )


def prep_kernel(
    per_group, share, place_ref, basis_hbm, inv_hbm, x_hbm, slots_ref,
    crem_hbm, y_hbm, bext_hbm, pos_ref, rest_ref, r_ref, btrem_ref, lines_ref,
    ccat, bt, basis_ref, y_ref, bext_ref, order_ref, inv_ref, square, x_ref, sems,
):
    basis_in = copy(basis_hbm, basis_ref, sems.at[0])
    held = jnp.minimum(place_ref[0] * share, inv_hbm.shape[0] - share)
    inv_in = copy(inv_hbm.at[pl.ds(held, share)], inv_ref, sems.at[4])
    x_in = copy(x_hbm, x_ref, sems.at[5], 1)
    patches, patch_nodes = slots_ref.shape
    waves, width = basis_ref.shape[1], basis_ref.shape[2]
    parts, nodes, _ = x_ref.shape
    core = nodes // patches
    rest = patch_nodes - core
    ext = ccat.shape[1]
    slots = slots_ref[...].astype(F32)
    first = (iota((patches, patch_nodes), 0) * core).astype(F32)
    local = slots - first
    outside = (local < 0.0) | (local >= float(core))
    before = iota((patch_nodes, patch_nodes), 0) < iota((patch_nodes, patch_nodes), 1)
    rank = dot(outside.astype(F32).astype(BF16), before.astype(F32).astype(BF16))
    pos = jnp.where(outside, rank + float(core), local)
    pos_ref[...] = pos
    for p in range(patches):
        prow = pos[p : p + 1, :]
        order_ref[p] = one_hot_rows(as_column(prow), patch_nodes)
        hit = prow == (iota((rest, patch_nodes), 0) + core).astype(F32)
        ids = jnp.sum(
            jnp.where(hit, jnp.broadcast_to(slots[p : p + 1, :], hit.shape), 0.0),
            axis=1,
            keepdims=True,
        )
        ids = jnp.broadcast_to(ids, (rest, LANES))
        rest_ref[:, p * rest : (p + 1) * rest] = jnp.transpose(ids)[0:8]
        ccat[p * rest : (p + 1) * rest, :] = one_hot_rows(ids, ext)
    basis_in.wait()
    for p in range(patches):
        basis = jnp.concatenate(
            [
                basis_ref[p, w, :, q * patch_nodes : (q + 1) * patch_nodes]
                for w in range(waves)
                for q in range(2)
            ],
            axis=0,
        )
        moved = dot(basis, order_ref[p]).astype(BF16)
        spread = dot(moved[:, core:], ccat[p * rest : (p + 1) * rest, :]).astype(BF16)
        for k in range(parts):
            rows = slice(k * width, (k + 1) * width)
            here = slice(p * width, (p + 1) * width)
            bt[k, here, :] = spread[rows]
            bt[k, here, p * core : (p + 1) * core] = (
                spread[rows, p * core : (p + 1) * core] + moved[rows, :core]
            )
    for k in range(parts):
        btrem_ref[k] = bt[k, :, nodes:]
        bext_ref[k] = jnp.transpose(bt[k])
    sent = [
        copy(ccat.at[:, pl.ds(nodes, ext - nodes)], crem_hbm, sems.at[1]),
        copy(bext_ref, bext_hbm, sems.at[3], 1),
    ]
    x_in.wait()
    for k in range(0, parts, 2):
        both = dot(ccat[:, :nodes], beside([x_ref[k], x_ref[k + 1]])).astype(BF16)
        for j in range(2):
            y_ref[k + j] = both[:, j * x_ref.shape[2] : (j + 1) * x_ref.shape[2]]
    inv_in.wait()
    lines_ref[...] = jnp.zeros(lines_ref.shape, F32)
    for w in range(waves):
        for t in range(share):
            square[...] = inv_ref[t, w].astype(F32)
            for c in range(per_group):
                lines_ref[w * share + t, :, c * width : (c + 1) * width] = square[
                    pl.ds(c, width // per_group, stride=per_group), :
                ]
    sent.append(copy(y_ref, y_hbm, sems.at[2]))
    for w in range(waves):
        r_ref[w] = sum(dot(bt[k, :, :nodes], x_ref[k]) for k in (2 * w, 2 * w + 1))
    for moved in sent:
        moved.wait()


def prepare(slots, basis_t, coarse_inv, x4, ext, per_group, share):
    parts, nodes, width = x4.shape
    patches, patch_nodes = slots.shape
    rest = patch_nodes - nodes // patches
    columns = patches * basis_t.shape[2]
    y = ((parts, patches * rest, width), BF16)
    b_ext = ((parts, ext, columns), BF16)
    size = coarse_inv.shape[3]
    waves = coarse_inv.shape[1]
    assert coarse_inv.shape[0] % share == 0
    return call(
        functools.partial(prep_kernel, per_group, share),
        20,
        [lax.axis_index("patch").astype(jnp.int32).reshape(1)],
        [basis_t, coarse_inv, x4],
        [slots],
        [((patches * rest, ext - nodes), BF16), y, b_ext],
        [
            ((patches, patch_nodes), F32),
            ((8, patches * rest), F32),
            ((parts // 2, columns, width), F32),
            ((parts, columns, ext - nodes), BF16),
            ((waves * share, size // per_group, LANES), F32),
        ],
        [
            vmem((patches * rest, ext), BF16),
            vmem((parts, columns, ext), BF16),
            vmem(basis_t.shape, BF16),
            vmem(*y),
            vmem(*b_ext),
            vmem((patches, patch_nodes, patch_nodes), BF16),
            vmem((share,) + coarse_inv.shape[1:], BF16),
            vmem((size, size), F32),
            vmem(x4.shape, BF16),
            pltpu.SemaphoreType.DMA((6,)),
        ],
    )


def owner_order(columns, patches, width, per_group):
    rows = patches * per_group
    i = iota((columns, columns), 0)
    j = iota((columns, columns), 1)
    source = ((i % rows) // per_group) * width + (i // rows) * per_group + i % per_group
    return (source == j).astype(F32).astype(BF16)


def restrict_kernel(
    per_group, block_ref, odd_ref, r_ref, btrem_ref, near_ref, other_ref, lines_ref,
    far_hbm, out_hbm, out_ref, sems,
):
    waves, columns, width = r_ref.shape
    patches = block_ref.shape[0]
    slots = near_ref.shape[1]
    rows = patches * per_group
    groups = columns // rows
    halves = width // LANES
    odd = odd_ref[0]
    sent = [
        copy(near_ref, far_hbm.at[:, pl.ds(pl.multiple_of((1 - odd) * slots, slots), slots)], sems.at[0]),
        copy(other_ref, far_hbm.at[:, pl.ds(pl.multiple_of(odd * slots, slots), slots)], sems.at[1]),
    ]
    order = owner_order(columns, patches, columns // patches, per_group)
    tail = out_ref.shape[1] - rows
    keys = jnp.zeros((tail, LANES), F32)
    for p in range(patches):
        keys = jnp.where(iota((tail, LANES), 0) == p, block_ref[p].astype(F32), keys)
    share = lines_ref.shape[0] // waves
    for w in range(waves):
        total = r_ref[w]
        for q in range(2):
            k = 2 * w + q
            near, other = near_ref[k], other_ref[k]
            total = total + dot(btrem_ref[k, :, :slots], jnp.where(odd == 0, other, near))
            total = total + dot(btrem_ref[k, :, slots:], jnp.where(odd == 0, near, other))
        moved = dot(order, total.astype(BF16)).astype(BF16)
        for g in range(groups):
            last = keys
            for t in range(share):
                line = jnp.broadcast_to(lines_ref[w * share + t, g : g + 1, :], keys.shape)
                last = jnp.where(iota((tail, LANES), 0) == patches + t, line, last)
            last = last.astype(BF16)
            for h in range(halves):
                owner = (w * groups + g) * halves + h
                out_ref[owner, :rows, :] = moved[g * rows : (g + 1) * rows, h * LANES : (h + 1) * LANES]
                out_ref[owner, rows:, :] = last
        part = pl.ds(w * groups * halves, groups * halves)
        sent.append(copy(out_ref.at[part], out_hbm.at[part], sems.at[2 + w], 1))
    for copied in sent:
        copied.wait()


def restrict(block, odd, r_own, bt_rem, near, other, lines, owners, per_group, padded):
    parts, slots, width = near.shape
    out = ((owners, padded, LANES), BF16)
    return call(
        functools.partial(restrict_kernel, per_group),
        3,
        [block, odd],
        [],
        [r_own, bt_rem, near, other, lines],
        [((parts, 2 * slots, width), BF16), out],
        [],
        [vmem(*out), pltpu.SemaphoreType.DMA((2 + r_own.shape[0],))],
    )


def sums_kernel(per_group, patches, coarse_count, blocks, share, got_ref, out_ref, data, tags):
    owners, padded, _ = got_ref.shape
    rows = patches * per_group
    tail = padded - rows
    for s in range(owners):
        data[s * rows : (s + 1) * rows, :] = got_ref[s, :rows, :].astype(F32)
        tags[s * tail : (s + 1) * tail, :] = got_ref[s, rows:, :].astype(F32)
    tag = tags[...].astype(BF16)
    count = owners * rows
    i = iota((count, owners * tail), 0)
    j = iota((count, owners * tail), 1)
    wanted = (i // rows) * tail + (i % rows) // per_group
    keys = dot((wanted == j).astype(F32).astype(BF16), tag)
    keys = keys * float(per_group) + (iota((count, LANES), 0) % per_group).astype(F32)
    key_row = jnp.transpose(keys)[0:1, :]
    column = jnp.concatenate([keys] * (count // LANES), axis=1)
    same = (column == key_row).astype(F32).astype(BF16)
    data[...] = dot(same, data[...].astype(BF16))

    pairs = owners * patches
    i = iota((pairs, owners * tail), 0)
    j = iota((pairs, owners * tail), 1)
    named = dot(((i // patches) * tail + i % patches == j).astype(F32).astype(BF16), tag)
    source, place = j // tail, j % tail - patches
    block = (source // coarse_count) * share + place
    held = (place >= 0) & (place < share) & (block < blocks)
    block = jnp.where(held, (source % coarse_count) * blocks + block, -1).astype(F32)
    if owners * tail >= LANES:
        named = jnp.concatenate([named] * (owners * tail // LANES), axis=1)
    tags[0:pairs, :] = dot((named == block).astype(F32).astype(BF16), tag)
    extra = out_ref.shape[1] - rows - patches
    for s in range(owners):
        out_ref[s, :rows, :] = data[s * rows : (s + 1) * rows, :].astype(BF16)
        last = tags[s * patches : (s + 1) * patches, :]
        if extra:
            last = jnp.concatenate([last, jnp.zeros((extra, LANES), F32)], axis=0)
        out_ref[s, rows:, :] = last.astype(BF16)


def owner_sums(got, patches, per_group, blocks, share):
    owners, padded, _ = got.shape
    rows = patches * per_group
    back = -(-(rows + patches) // 8) * 8
    out = ((owners, back, LANES), BF16)
    return call(
        functools.partial(
            sums_kernel, per_group, patches, lax.axis_size("coarse"), blocks, share
        ),
        6,
        [],
        [],
        [got],
        [],
        [out],
        [
            vmem((owners * rows, LANES), F32),
            vmem((owners * (padded - rows), LANES), F32),
        ],
    )[0]


def local_kernel(
    first, inv_hbm, x_hbm, y_hbm, crem_hbm, far_hbm, pos_ref,
    local_hbm, rest_hbm,
    g, inv_ref, x_ref, y_ref, crem_ref, far_ref, local_ref, rest_ref, order_ref, back_ref,
    sems, inv_sems, out_sems,
):
    parts, rows, width = x_ref.shape
    count, waves = inv_ref.shape[:2]
    patch_nodes = pos_ref.shape[1]
    core = rows // count
    rest = patch_nodes - core
    mine = pl.ds(first * rest, count * rest)
    small = [
        copy(crem_hbm.at[mine], crem_ref, sems.at[0]),
        copy(far_hbm, far_ref, sems.at[1]),
        copy(y_hbm.at[:, mine], y_ref, sems.at[2]),
        copy(x_hbm.at[:, pl.ds(first * core, rows)], x_ref, sems.at[3]),
    ]
    inverses = {
        (i, w): copy(inv_hbm.at[first + i, w], inv_ref.at[i, w], inv_sems.at[i * waves + w], 1)
        for i in range(count)
        for w in range(waves)
    }
    for i in range(count):
        prow = pos_ref[first + i : first + i + 1, :]
        order_ref[i] = one_hot_rows(as_column(prow), patch_nodes)
        places = (iota((rest, patch_nodes), 0) + core).astype(F32)
        back_ref[i] = (prow == places).astype(F32).astype(BF16)
    for moved in small:
        moved.wait()
    for i in range(count):
        here = slice(i * rest, (i + 1) * rest)
        for k in range(0, parts, 2):
            far = dot(crem_ref[here, :], beside([far_ref[k], far_ref[k + 1]]))
            other = beside([y_ref[k, here, :], y_ref[k + 1, here, :]]) + far.astype(BF16)
            rows = slice(i * core, (i + 1) * core)
            mine = beside([x_ref[k, rows, :], x_ref[k + 1, rows, :]])
            moved = dot(order_ref[i], jnp.concatenate([mine, other], axis=0)).astype(BF16)
            for j in range(2):
                at = (k + j) * patch_nodes
                g[i, at : at + patch_nodes, :] = moved[:, j * width : (j + 1) * width]
    sent = []
    for i in range(count):
        here = slice(i * rest, (i + 1) * rest)
        for w in range(waves):
            inverses[i, w].wait()
        for w in range(waves):
            terms = g[i, 2 * w * patch_nodes : 2 * (w + 1) * patch_nodes, :]
            local_ref[i, w] = dot_in_halves(inv_ref.at[i, w], terms).astype(BF16)
        sent.append(copy(local_ref.at[i], local_hbm.at[i], out_sems.at[i]))
        for w in range(waves):
            pair = beside([local_ref[i, w, :patch_nodes, :], local_ref[i, w, patch_nodes:, :]])
            got = dot(back_ref[i], pair).astype(BF16)
            for j in range(2):
                rest_ref[2 * w + j, here, :] = got[:, j * width : (j + 1) * width]
    sent.append(copy(rest_ref, rest_hbm, sems.at[0]))
    for moved in sent:
        moved.wait()


def local_products(pos, x4, y, crem, far, patch_inv, first, count):
    parts, nodes, width = x4.shape
    patches, patch_nodes = pos.shape
    core = nodes // patches
    rest = patch_nodes - core
    waves = patch_inv.shape[1]
    local = ((count, waves, 2 * patch_nodes, width), BF16)
    others = ((parts, count * rest, width), BF16)
    return call(
        functools.partial(local_kernel, first),
        24,
        [],
        [patch_inv, x4, y, crem, far],
        [pos],
        [local, others],
        [],
        [
            vmem((count, parts * patch_nodes, width), BF16),
            vmem((count,) + patch_inv.shape[1:], BF16),
            vmem((parts, count * core, width), BF16),
            vmem(*others),
            vmem((count * rest, crem.shape[1]), BF16),
            vmem((parts, crem.shape[1], width), BF16),
            vmem(*local),
            vmem(*others),
            vmem((count, patch_nodes, patch_nodes), BF16),
            vmem((count, rest, patch_nodes), BF16),
            pltpu.SemaphoreType.DMA((4,)),
            pltpu.SemaphoreType.DMA((count * waves,)),
            pltpu.SemaphoreType.DMA((count,)),
        ],
    )


def coef_kernel(
    per_group, patches, odd_ref, bext_hbm, *refs
):
    *other_hbm, sums_ref, rest_ref, coef_ref, near_ref, far_ref = refs[:-5]
    gathered, inverses, brem_ref, other_ref, sems = refs[-5:]
    slots = near_ref.shape[1]
    nodes = bext_hbm.shape[1] - 2 * slots
    odd = odd_ref[0]
    starts = [pl.multiple_of(nodes + h * slots, slots) for h in (1 - odd, odd)]
    arriving = [
        copy(
            bext_hbm.at[:, pl.ds(start, slots)],
            brem_ref.at[:, pl.ds(h * slots, slots)],
            sems.at[h],
        )
        for h, start in enumerate(starts)
    ]
    start = 0
    for i, other in enumerate(other_hbm):
        place = pl.ds(start, other.shape[1])
        arriving.append(copy(other, other_ref.at[:, place], sems.at[2 + i], 1))
        start += other.shape[1]
    waves, columns, width = coef_ref.shape
    size = columns // patches
    rows = patches * per_group
    groups = columns // rows
    halves = width // LANES
    held = groups * patches
    i = iota((columns, held), 0)
    j = iota((columns, held), 1)
    grow = ((i % size) // per_group * patches + i // size == j).astype(F32).astype(BF16)
    in_lanes = iota((columns, LANES), 1) // size == iota((columns, LANES), 0) % per_group
    i = iota((LANES, columns), 0)
    j = iota((LANES, columns), 1)
    fold = (i % size == (j // rows) * per_group + j % per_group).astype(F32).astype(BF16)
    i = iota((columns, columns), 0)
    j = iota((columns, columns), 1)
    in_patch = (j % rows) // per_group == i // size
    ids = rest_ref[0:1, :]
    reach = (2 * slots, ids.shape[1])
    row = iota(reach, 0)
    swap = jnp.where(odd == 0, slots, 0)
    place = jnp.where(row < slots, row + swap, row - swap) + nodes
    spread = (ids == place.astype(F32)).astype(F32).astype(BF16)
    for w in range(waves):
        for g in range(groups):
            for h in range(halves):
                owner = (w * groups + g) * halves + h
                gathered[g * rows : (g + 1) * rows, h * LANES : (h + 1) * LANES] = sums_ref[
                    owner, :rows, :
                ].astype(F32)
            inverses[g * patches : (g + 1) * patches, :] = sums_ref[
                (w * groups + g) * halves, rows : rows + patches, :
            ].astype(F32)
        grown = dot(grow, inverses[...].astype(BF16))
        folded = dot(jnp.where(in_lanes, grown, 0.0).astype(BF16), fold)
        inverse = jnp.where(in_patch, folded, 0.0).astype(BF16)
        coef = dot(inverse, gathered[...].astype(BF16)).astype(BF16)
        coef_ref[w] = coef
        if w == 0:
            for moved in arriving:
                moved.wait()
        for q in range(2):
            k = 2 * w + q
            margin = (dot(spread, other_ref[k]) + dot(brem_ref[k], coef)).astype(BF16)
            near_ref[k] = margin[:slots]
            far_ref[k] = margin[slots:]


def coefficients(odd, sums, b_ext, rest_ids, others, patches, slots, per_group):
    parts, _, columns = b_ext.shape
    width = others[0].shape[2]
    groups = columns // (patches * per_group)
    margin = ((parts, slots, width), BF16)
    return call(
        functools.partial(coef_kernel, per_group, patches),
        6,
        [odd],
        [b_ext] + others,
        [sums, rest_ids],
        [],
        [((parts // 2, columns, width), BF16), margin, margin],
        [
            vmem((columns, width), F32),
            vmem((groups * patches, LANES), F32),
            vmem((parts, 2 * slots, columns), BF16),
            vmem((parts, rest_ids.shape[1], width), BF16),
            pltpu.SemaphoreType.DMA((2 + len(others),)),
        ],
    )


def own_kernel(odd_ref, bext_hbm, *refs):
    *pairs, rows_ref, rest_ref, pos_ref, coef_ref, out_ref, back_ref, bown_ref, local_ref, other_ref, sems = refs
    half = len(pairs) // 2
    parts, nodes, _ = out_ref.shape
    patches, patch_nodes = pos_ref.shape
    core = nodes // patches
    def load(k):
        moves = [(bext_hbm.at[k, pl.ds(0, nodes)], bown_ref.at[k])]
        start = 0
        for a in pairs[half:]:
            moves.append((a.at[k], other_ref.at[k, pl.ds(start, a.shape[1])]))
            start += a.shape[1]
        start = 0
        terms = pl.ds((k % 2) * patch_nodes, patch_nodes)
        for a in pairs[:half]:
            here = pl.ds(start, a.shape[0])
            moves.append((a.at[:, k // 2, terms], local_ref.at[k, here]))
            start += a.shape[0]
        return [copy(m[0], m[1], sems.at[k, i], i % 2) for i, m in enumerate(moves)]

    arriving = {k: load(k) for k in range(2)}
    slots = rows_ref.shape[1]
    for b, ids in enumerate(partner_rows(rows_ref, odd_ref[0])):
        back_ref[:, b * slots : (b + 1) * slots] = (
            (ids == iota((nodes, slots), 0).astype(F32)).astype(F32).astype(BF16)
        )
    ids = rest_ref[0:1, :]
    shape = (nodes, ids.shape[1])
    spread = (ids == iota(shape, 0).astype(F32)).astype(F32).astype(BF16)
    places = iota((core, patch_nodes), 0).astype(F32)
    backs = [
        (pos_ref[p : p + 1, :] == places).astype(F32).astype(BF16) for p in range(patches)
    ]
    width = out_ref.shape[2]
    for k in range(0, parts, 2):
        for moved in arriving[k] + arriving[k + 1]:
            moved.wait()
        for later in range(k + 2, min(k + 4, parts)):
            arriving[later] = load(later)
        total = dot(spread, beside([other_ref[k], other_ref[k + 1]]))
        cores = [
            dot(backs[p], beside([local_ref[k, p], local_ref[k + 1, p]])) for p in range(patches)
        ]
        total = total + jnp.concatenate(cores, axis=0)
        for j in range(2):
            coarse = dot(bown_ref[k + j], coef_ref[(k + j) // 2])
            out_ref[k + j] = total[:, j * width : (j + 1) * width] + coarse


def own_rows(odd, b_ext, coef, rows, rest_ids, pos, locals_, others, nodes):
    parts, _, columns = b_ext.shape
    width = coef.shape[2]
    return call(
        own_kernel,
        20,
        [odd],
        [b_ext] + locals_ + others,
        [rows, rest_ids, pos, coef],
        [],
        [((parts, nodes, width), F32), ((nodes, 2 * rows.shape[1]), BF16)],
        [
            vmem((parts, nodes, columns), BF16),
            vmem((parts,) + pos.shape + (width,), BF16),
            vmem((parts, rest_ids.shape[1], width), BF16),
            pltpu.SemaphoreType.DMA((parts, 1 + len(locals_) + len(others))),
        ],
    )


def final_kernel(own_ref, spread_ref, near_ref, other_ref, out_hbm, out_ref, sems):
    parts, _, width = own_ref.shape
    sent = []
    for k in range(0, parts, 2):
        back = jnp.concatenate(
            [beside([a[k], a[k + 1]]) for a in (near_ref, other_ref)], axis=0
        )
        total = dot(spread_ref[...], back)
        for j in range(2):
            mine = total[:, j * width : (j + 1) * width]
            out_ref[k + j] = (own_ref[k + j] + mine).astype(BF16)
            sent.append(copy(out_ref.at[k + j], out_hbm.at[k + j], sems.at[k + j], j))
    for moved in sent:
        moved.wait()


def finish(own, spread, near, other):
    return call(
        final_kernel,
        12,
        [],
        [],
        [own, spread, near, other],
        [(own.shape, BF16)],
        [],
        [vmem(own.shape, BF16), pltpu.SemaphoreType.DMA((own.shape[0],))],
    )[0]


def per_device(residual, patch_inv, coarse_basis, coarse_inv, patch_slots, send_rows, coarse_block):
    waves, _, nodes, width = residual.shape
    patches = patch_inv.shape[0]
    size = coarse_basis.shape[3]
    slots = send_rows.shape[2]
    ext = nodes + 2 * slots
    owners = lax.axis_size(AXES)
    halves = width // LANES
    groups = owners // (waves * halves)
    per_group = size // groups
    assert owners % 2 == 0 and groups * waves * halves == owners and per_group * groups == size
    blocks = coarse_inv.shape[0]
    share = -(-blocks // lax.axis_size("patch"))
    rows = patches * per_group
    padded = -(-(rows + patches + share) // 8) * 8
    half = patches // 2
    send = send_rows[0]
    odd = (lax.axis_index(AXES) % 2).astype(jnp.int32).reshape(1)
    basis_t = jnp.swapaxes(coarse_basis, 2, 3)

    x_all = residual.reshape(2 * waves, nodes, width)
    to_first, to_second, slots_v = select_rows(x_all, send, patch_slots, odd)
    first_rows = swapped(to_first, AXES, False)
    second_rows = swapped(to_second, AXES, True)
    crem, y, b_ext, pos, rest_ids, r_own, bt_rem, lines = prepare(
        slots_v, basis_t, coarse_inv, x_all, ext, per_group, share
    )
    far, sent = restrict(
        coarse_block, odd, r_own, bt_rem, first_rows, second_rows, lines,
        owners, per_group, padded,
    )
    got = lax.all_to_all(sent, AXES, 0, 0, tiled=True)
    local_a, rest_a = local_products(pos, x_all, y, crem, far, patch_inv, 0, half)
    sums = owner_sums(got, patches, per_group, blocks, share)
    mine = lax.all_to_all(sums, AXES, 0, 0, tiled=True)
    local_b, rest_b = local_products(pos, x_all, y, crem, far, patch_inv, half, patches - half)
    coef, to_first, to_second = coefficients(
        odd, mine, b_ext, rest_ids, [rest_a, rest_b], patches, slots, per_group
    )
    first_back = swapped(to_first, AXES, False)
    second_back = swapped(to_second, AXES, True)
    own, spread = own_rows(odd, b_ext, coef, send, rest_ids, pos, [local_a, local_b], [rest_a, rest_b], nodes)
    out = finish(own, spread, first_back, second_back)
    return out.reshape(residual.shape)


def solution(mesh):
    placed = (
        P(None, None, AXES, None),
        P(AXES, None, None, None),
        P(AXES, None, None, None),
        P("coarse", None, None, None),
        P(AXES, None),
        P(AXES, None, None),
        P(AXES),
    )
    return jax.shard_map(
        per_device,
        mesh=mesh,
        in_specs=placed,
        out_specs=P(None, None, AXES, None),
        check_vma=False,
    )
```

```python
import functools

import jax
import jax.numpy as jnp
from jax import lax
from jax.experimental import pallas as pl
from jax.experimental.pallas import tpu as pltpu
from jax.sharding import PartitionSpec as P


AXES = ("patch", "coarse")
LANES = 128
MIB = 1 << 20
F32 = jnp.float32
BF16 = jnp.bfloat16


def swapped(value, axis, odd_first):
    count = lax.axis_size(axis)
    shift = int(odd_first)
    partner = {(i + shift) % count: ((i ^ 1) + shift) % count for i in range(count)}
    return lax.ppermute(value, axis, sorted(partner.items()))


def dot(a, b):
    return jnp.dot(a, b, preferred_element_type=F32)


def beside(parts):
    return jnp.concatenate(parts, axis=1)


def dot_in_halves(a_ref, b):
    half = b.shape[0] // 2
    return dot(a_ref[:, :half], b[:half]) + dot(a_ref[:, half:], b[half:])


def as_column(row):
    return jnp.transpose(jnp.broadcast_to(row, (LANES, row.shape[1])))


def iota(shape, axis):
    return lax.broadcasted_iota(jnp.int32, shape, axis)


def one_hot_rows(column, width, start=0):
    rows = column.shape[0]
    parts = [
        (column == (iota((rows, LANES), 1) + (start + t)).astype(F32)).astype(F32).astype(BF16)
        for t in range(0, width, LANES)
    ]
    return jnp.concatenate(parts, axis=1)


def vmem(shape, dtype):
    return pltpu.VMEM(shape, dtype)


def resident(array):
    return pltpu.with_memory_space_constraint(array, pltpu.VMEM)


def call(kernel, limit, smem, far, near, far_out, near_out, scratch=()):
    spaces = [pltpu.SMEM] * len(smem) + [pltpu.HBM] * len(far) + [pltpu.VMEM] * len(near)
    out_spaces = [pltpu.HBM] * len(far_out) + [pltpu.VMEM] * len(near_out)
    return pl.pallas_call(
        kernel,
        in_specs=[pl.BlockSpec(memory_space=m) for m in spaces],
        out_specs=[pl.BlockSpec(memory_space=m) for m in out_spaces],
        out_shape=[pltpu.HBM(*o) for o in far_out] + [vmem(*o) for o in near_out],
        scratch_shapes=list(scratch),
        compiler_params=pltpu.CompilerParams(vmem_limit_bytes=limit * MIB),
    )(
        *smem,
        *[pltpu.with_memory_space_constraint(a, pltpu.HBM) for a in far],
        *[resident(a) for a in near],
    )


def copy(source, target, sem, priority=0):
    moved = pltpu.make_async_copy(source, target, sem)
    moved.start(priority=priority)
    return moved


def partner_rows(rows_ref, odd):
    up, down = (rows_ref[b : b + 1, :].astype(F32) for b in range(2))
    return jnp.where(odd == 0, up, down), jnp.where(odd == 0, down, up)


def select_kernel(
    odd_ref, x_hbm, rows_hbm, slots_hbm, near_ref, far_ref, slots_ref,
    x_ref, rows_ref, arrived,
):
    slots = rows_ref.shape[1]
    parts, nodes, _ = x_ref.shape
    small = pltpu.make_async_copy(rows_hbm, rows_ref, arrived.at[parts])
    copies = [pltpu.make_async_copy(x_hbm.at[k], x_ref.at[k], arrived.at[k]) for k in range(parts)]
    later = pltpu.make_async_copy(slots_hbm, slots_ref, arrived.at[parts + 1])
    for i, moved in enumerate([small] + copies + [later]):
        moved.start(priority=i % 2)
    small.wait()
    pick = jnp.concatenate(
        [one_hot_rows(as_column(ids), nodes) for ids in partner_rows(rows_ref, odd_ref[0])], axis=0
    )
    width = x_ref.shape[2]
    for k in range(0, parts, 2):
        copies[k].wait()
        copies[k + 1].wait()
        got = dot(pick, beside([x_ref[k], x_ref[k + 1]])).astype(BF16)
        for j in range(2):
            near_ref[k + j] = got[:slots, j * width : (j + 1) * width]
            far_ref[k + j] = got[slots:, j * width : (j + 1) * width]
    later.wait()


def select_rows(x4, rows, patch_slots, odd):
    parts, _, width = x4.shape
    margin = ((parts, rows.shape[1], width), BF16)
    return call(
        select_kernel,
        10,
        [odd],
        [x4, rows, patch_slots],
        [],
        [],
        [margin, margin, (patch_slots.shape, patch_slots.dtype)],
        [vmem(x4.shape, BF16), vmem(rows.shape, rows.dtype), pltpu.SemaphoreType.DMA((parts + 2,))],
    )


def prep_kernel(
    per_group, share, place_ref, basis_hbm, inv_hbm, x_hbm, slots_ref,
    crem_hbm, y_hbm, bext_hbm, pos_ref, rest_ref, r_ref, btrem_ref, lines_ref,
    ccat, bt, basis_ref, y_ref, bext_ref, order_ref, inv_ref, square, x_ref, sems,
):
    basis_in = copy(basis_hbm, basis_ref, sems.at[0])
    held = jnp.minimum(place_ref[0] * share, inv_hbm.shape[0] - share)
    inv_in = copy(inv_hbm.at[pl.ds(held, share)], inv_ref, sems.at[4])
    x_in = copy(x_hbm, x_ref, sems.at[5], 1)
    patches, patch_nodes = slots_ref.shape
    waves, width = basis_ref.shape[1], basis_ref.shape[2]
    parts, nodes, _ = x_ref.shape
    core = nodes // patches
    rest = patch_nodes - core
    ext = ccat.shape[1]
    slots = slots_ref[...].astype(F32)
    first = (iota((patches, patch_nodes), 0) * core).astype(F32)
    local = slots - first
    outside = (local < 0.0) | (local >= float(core))
    before = iota((patch_nodes, patch_nodes), 0) < iota((patch_nodes, patch_nodes), 1)
    rank = dot(outside.astype(F32).astype(BF16), before.astype(F32).astype(BF16))
    pos = jnp.where(outside, rank + float(core), local)
    pos_ref[...] = pos
    for p in range(patches):
        prow = pos[p : p + 1, :]
        order_ref[p] = one_hot_rows(as_column(prow), patch_nodes)
        hit = prow == (iota((rest, patch_nodes), 0) + core).astype(F32)
        ids = jnp.sum(
            jnp.where(hit, jnp.broadcast_to(slots[p : p + 1, :], hit.shape), 0.0),
            axis=1,
            keepdims=True,
        )
        ids = jnp.broadcast_to(ids, (rest, LANES))
        rest_ref[:, p * rest : (p + 1) * rest] = jnp.transpose(ids)[0:8]
        ccat[p * rest : (p + 1) * rest, :] = one_hot_rows(ids, ext)
    basis_in.wait()
    for p in range(patches):
        basis = jnp.concatenate(
            [
                basis_ref[p, w, :, q * patch_nodes : (q + 1) * patch_nodes]
                for w in range(waves)
                for q in range(2)
            ],
            axis=0,
        )
        moved = dot(basis, order_ref[p]).astype(BF16)
        spread = dot(moved[:, core:], ccat[p * rest : (p + 1) * rest, :]).astype(BF16)
        for k in range(parts):
            rows = slice(k * width, (k + 1) * width)
            here = slice(p * width, (p + 1) * width)
            bt[k, here, :] = spread[rows]
            bt[k, here, p * core : (p + 1) * core] = (
                spread[rows, p * core : (p + 1) * core] + moved[rows, :core]
            )
    for k in range(parts):
        btrem_ref[k] = bt[k, :, nodes:]
        bext_ref[k] = jnp.transpose(bt[k])
    sent = [
        copy(ccat.at[:, pl.ds(nodes, ext - nodes)], crem_hbm, sems.at[1]),
        copy(bext_ref, bext_hbm, sems.at[3], 1),
    ]
    x_in.wait()
    for k in range(0, parts, 2):
        both = dot(ccat[:, :nodes], beside([x_ref[k], x_ref[k + 1]])).astype(BF16)
        for j in range(2):
            y_ref[k + j] = both[:, j * x_ref.shape[2] : (j + 1) * x_ref.shape[2]]
    inv_in.wait()
    lines_ref[...] = jnp.zeros(lines_ref.shape, F32)
    for w in range(waves):
        for t in range(share):
            square[...] = inv_ref[t, w].astype(F32)
            for c in range(per_group):
                lines_ref[w * share + t, :, c * width : (c + 1) * width] = square[
                    pl.ds(c, width // per_group, stride=per_group), :
                ]
    sent.append(copy(y_ref, y_hbm, sems.at[2]))
    for w in range(waves):
        r_ref[w] = sum(dot(bt[k, :, :nodes], x_ref[k]) for k in (2 * w, 2 * w + 1))
    for moved in sent:
        moved.wait()


def prepare(slots, basis_t, coarse_inv, x4, ext, per_group, share):
    parts, nodes, width = x4.shape
    patches, patch_nodes = slots.shape
    rest = patch_nodes - nodes // patches
    columns = patches * basis_t.shape[2]
    y = ((parts, patches * rest, width), BF16)
    b_ext = ((parts, ext, columns), BF16)
    size = coarse_inv.shape[3]
    waves = coarse_inv.shape[1]
    assert coarse_inv.shape[0] % share == 0
    return call(
        functools.partial(prep_kernel, per_group, share),
        20,
        [lax.axis_index("patch").astype(jnp.int32).reshape(1)],
        [basis_t, coarse_inv, x4],
        [slots],
        [((patches * rest, ext - nodes), BF16), y, b_ext],
        [
            ((patches, patch_nodes), F32),
            ((8, patches * rest), F32),
            ((parts // 2, columns, width), F32),
            ((parts, columns, ext - nodes), BF16),
            ((waves * share, size // per_group, LANES), F32),
        ],
        [
            vmem((patches * rest, ext), BF16),
            vmem((parts, columns, ext), BF16),
            vmem(basis_t.shape, BF16),
            vmem(*y),
            vmem(*b_ext),
            vmem((patches, patch_nodes, patch_nodes), BF16),
            vmem((share,) + coarse_inv.shape[1:], BF16),
            vmem((size, size), F32),
            vmem(x4.shape, BF16),
            pltpu.SemaphoreType.DMA((6,)),
        ],
    )


def owner_order(columns, patches, width, per_group):
    rows = patches * per_group
    i = iota((columns, columns), 0)
    j = iota((columns, columns), 1)
    source = ((i % rows) // per_group) * width + (i // rows) * per_group + i % per_group
    return (source == j).astype(F32).astype(BF16)


def restrict_kernel(
    per_group, block_ref, odd_ref, r_ref, btrem_ref, near_ref, other_ref, lines_ref,
    far_hbm, out_hbm, out_ref, sems,
):
    waves, columns, width = r_ref.shape
    patches = block_ref.shape[0]
    slots = near_ref.shape[1]
    rows = patches * per_group
    groups = columns // rows
    halves = width // LANES
    odd = odd_ref[0]
    sent = [
        copy(near_ref, far_hbm.at[:, pl.ds(pl.multiple_of((1 - odd) * slots, slots), slots)], sems.at[0]),
        copy(other_ref, far_hbm.at[:, pl.ds(pl.multiple_of(odd * slots, slots), slots)], sems.at[1]),
    ]
    order = owner_order(columns, patches, columns // patches, per_group)
    tail = out_ref.shape[1] - rows
    keys = jnp.zeros((tail, LANES), F32)
    for p in range(patches):
        keys = jnp.where(iota((tail, LANES), 0) == p, block_ref[p].astype(F32), keys)
    share = lines_ref.shape[0] // waves
    for w in range(waves):
        total = r_ref[w]
        for q in range(2):
            k = 2 * w + q
            near, other = near_ref[k], other_ref[k]
            total = total + dot(btrem_ref[k, :, :slots], jnp.where(odd == 0, other, near))
            total = total + dot(btrem_ref[k, :, slots:], jnp.where(odd == 0, near, other))
        moved = dot(order, total.astype(BF16)).astype(BF16)
        for g in range(groups):
            last = keys
            for t in range(share):
                line = jnp.broadcast_to(lines_ref[w * share + t, g : g + 1, :], keys.shape)
                last = jnp.where(iota((tail, LANES), 0) == patches + t, line, last)
            last = last.astype(BF16)
            for h in range(halves):
                owner = (w * groups + g) * halves + h
                out_ref[owner, :rows, :] = moved[g * rows : (g + 1) * rows, h * LANES : (h + 1) * LANES]
                out_ref[owner, rows:, :] = last
        part = pl.ds(w * groups * halves, groups * halves)
        sent.append(copy(out_ref.at[part], out_hbm.at[part], sems.at[2 + w], 1))
    for copied in sent:
        copied.wait()


def restrict(block, odd, r_own, bt_rem, near, other, lines, owners, per_group, padded):
    parts, slots, width = near.shape
    out = ((owners, padded, LANES), BF16)
    return call(
        functools.partial(restrict_kernel, per_group),
        3,
        [block, odd],
        [],
        [r_own, bt_rem, near, other, lines],
        [((parts, 2 * slots, width), BF16), out],
        [],
        [vmem(*out), pltpu.SemaphoreType.DMA((2 + r_own.shape[0],))],
    )


def sums_kernel(per_group, patches, coarse_count, blocks, share, got_ref, out_ref, data, tags):
    owners, padded, _ = got_ref.shape
    rows = patches * per_group
    tail = padded - rows
    for s in range(owners):
        data[s * rows : (s + 1) * rows, :] = got_ref[s, :rows, :].astype(F32)
        tags[s * tail : (s + 1) * tail, :] = got_ref[s, rows:, :].astype(F32)
    tag = tags[...].astype(BF16)
    count = owners * rows
    i = iota((count, owners * tail), 0)
    j = iota((count, owners * tail), 1)
    wanted = (i // rows) * tail + (i % rows) // per_group
    keys = dot((wanted == j).astype(F32).astype(BF16), tag)
    keys = keys * float(per_group) + (iota((count, LANES), 0) % per_group).astype(F32)
    key_row = jnp.transpose(keys)[0:1, :]
    column = jnp.concatenate([keys] * (count // LANES), axis=1)
    same = (column == key_row).astype(F32).astype(BF16)
    data[...] = dot(same, data[...].astype(BF16))

    pairs = owners * patches
    i = iota((pairs, owners * tail), 0)
    j = iota((pairs, owners * tail), 1)
    named = dot(((i // patches) * tail + i % patches == j).astype(F32).astype(BF16), tag)
    source, place = j // tail, j % tail - patches
    block = (source // coarse_count) * share + place
    held = (place >= 0) & (place < share) & (block < blocks)
    block = jnp.where(held, (source % coarse_count) * blocks + block, -1).astype(F32)
    if owners * tail >= LANES:
        named = jnp.concatenate([named] * (owners * tail // LANES), axis=1)
    tags[0:pairs, :] = dot((named == block).astype(F32).astype(BF16), tag)
    extra = out_ref.shape[1] - rows - patches
    for s in range(owners):
        out_ref[s, :rows, :] = data[s * rows : (s + 1) * rows, :].astype(BF16)
        last = tags[s * patches : (s + 1) * patches, :]
        if extra:
            last = jnp.concatenate([last, jnp.zeros((extra, LANES), F32)], axis=0)
        out_ref[s, rows:, :] = last.astype(BF16)


def owner_sums(got, patches, per_group, blocks, share):
    owners, padded, _ = got.shape
    rows = patches * per_group
    back = -(-(rows + patches) // 8) * 8
    out = ((owners, back, LANES), BF16)
    return call(
        functools.partial(
            sums_kernel, per_group, patches, lax.axis_size("coarse"), blocks, share
        ),
        6,
        [],
        [],
        [got],
        [],
        [out],
        [
            vmem((owners * rows, LANES), F32),
            vmem((owners * (padded - rows), LANES), F32),
        ],
    )[0]


def local_kernel(
    first, inv_hbm, x_hbm, y_hbm, crem_hbm, far_hbm, pos_ref,
    local_hbm, rest_hbm,
    g, inv_ref, x_ref, y_ref, crem_ref, far_ref, local_ref, rest_ref, order_ref, back_ref,
    sems, inv_sems, out_sems,
):
    parts, rows, width = x_ref.shape
    count, waves = inv_ref.shape[:2]
    patch_nodes = pos_ref.shape[1]
    core = rows // count
    rest = patch_nodes - core
    mine = pl.ds(first * rest, count * rest)
    small = [
        copy(crem_hbm.at[mine], crem_ref, sems.at[0]),
        copy(far_hbm, far_ref, sems.at[1]),
        copy(y_hbm.at[:, mine], y_ref, sems.at[2]),
        copy(x_hbm.at[:, pl.ds(first * core, rows)], x_ref, sems.at[3]),
    ]
    inverses = {
        (i, w): copy(inv_hbm.at[first + i, w], inv_ref.at[i, w], inv_sems.at[i * waves + w], 1)
        for i in range(count)
        for w in range(waves)
    }
    for i in range(count):
        prow = pos_ref[first + i : first + i + 1, :]
        order_ref[i] = one_hot_rows(as_column(prow), patch_nodes)
        places = (iota((rest, patch_nodes), 0) + core).astype(F32)
        back_ref[i] = (prow == places).astype(F32).astype(BF16)
    for moved in small:
        moved.wait()
    for i in range(count):
        here = slice(i * rest, (i + 1) * rest)
        for k in range(0, parts, 2):
            far = dot(crem_ref[here, :], beside([far_ref[k], far_ref[k + 1]]))
            other = beside([y_ref[k, here, :], y_ref[k + 1, here, :]]) + far.astype(BF16)
            rows = slice(i * core, (i + 1) * core)
            mine = beside([x_ref[k, rows, :], x_ref[k + 1, rows, :]])
            moved = dot(order_ref[i], jnp.concatenate([mine, other], axis=0)).astype(BF16)
            for j in range(2):
                at = (k + j) * patch_nodes
                g[i, at : at + patch_nodes, :] = moved[:, j * width : (j + 1) * width]
    sent = []
    for i in range(count):
        here = slice(i * rest, (i + 1) * rest)
        for w in range(waves):
            inverses[i, w].wait()
        for w in range(waves):
            terms = g[i, 2 * w * patch_nodes : 2 * (w + 1) * patch_nodes, :]
            local_ref[i, w] = dot_in_halves(inv_ref.at[i, w], terms).astype(BF16)
        sent.append(copy(local_ref.at[i], local_hbm.at[i], out_sems.at[i]))
        for w in range(waves):
            pair = beside([local_ref[i, w, :patch_nodes, :], local_ref[i, w, patch_nodes:, :]])
            got = dot(back_ref[i], pair).astype(BF16)
            for j in range(2):
                rest_ref[2 * w + j, here, :] = got[:, j * width : (j + 1) * width]
    sent.append(copy(rest_ref, rest_hbm, sems.at[0]))
    for moved in sent:
        moved.wait()


def local_products(pos, x4, y, crem, far, patch_inv, first, count):
    parts, nodes, width = x4.shape
    patches, patch_nodes = pos.shape
    core = nodes // patches
    rest = patch_nodes - core
    waves = patch_inv.shape[1]
    local = ((count, waves, 2 * patch_nodes, width), BF16)
    others = ((parts, count * rest, width), BF16)
    return call(
        functools.partial(local_kernel, first),
        24,
        [],
        [patch_inv, x4, y, crem, far],
        [pos],
        [local, others],
        [],
        [
            vmem((count, parts * patch_nodes, width), BF16),
            vmem((count,) + patch_inv.shape[1:], BF16),
            vmem((parts, count * core, width), BF16),
            vmem(*others),
            vmem((count * rest, crem.shape[1]), BF16),
            vmem((parts, crem.shape[1], width), BF16),
            vmem(*local),
            vmem(*others),
            vmem((count, patch_nodes, patch_nodes), BF16),
            vmem((count, rest, patch_nodes), BF16),
            pltpu.SemaphoreType.DMA((4,)),
            pltpu.SemaphoreType.DMA((count * waves,)),
            pltpu.SemaphoreType.DMA((count,)),
        ],
    )


def coef_kernel(
    per_group, patches, odd_ref, bext_hbm, *refs
):
    *other_hbm, sums_ref, rest_ref, coef_ref, near_ref, far_ref = refs[:-5]
    gathered, inverses, brem_ref, other_ref, sems = refs[-5:]
    slots = near_ref.shape[1]
    nodes = bext_hbm.shape[1] - 2 * slots
    odd = odd_ref[0]
    starts = [pl.multiple_of(nodes + h * slots, slots) for h in (1 - odd, odd)]
    arriving = [
        copy(
            bext_hbm.at[:, pl.ds(start, slots)],
            brem_ref.at[:, pl.ds(h * slots, slots)],
            sems.at[h],
        )
        for h, start in enumerate(starts)
    ]
    start = 0
    for i, other in enumerate(other_hbm):
        place = pl.ds(start, other.shape[1])
        arriving.append(copy(other, other_ref.at[:, place], sems.at[2 + i], 1))
        start += other.shape[1]
    waves, columns, width = coef_ref.shape
    size = columns // patches
    rows = patches * per_group
    groups = columns // rows
    halves = width // LANES
    held = groups * patches
    i = iota((columns, held), 0)
    j = iota((columns, held), 1)
    grow = ((i % size) // per_group * patches + i // size == j).astype(F32).astype(BF16)
    in_lanes = iota((columns, LANES), 1) // size == iota((columns, LANES), 0) % per_group
    i = iota((LANES, columns), 0)
    j = iota((LANES, columns), 1)
    fold = (i % size == (j // rows) * per_group + j % per_group).astype(F32).astype(BF16)
    i = iota((columns, columns), 0)
    j = iota((columns, columns), 1)
    in_patch = (j % rows) // per_group == i // size
    ids = rest_ref[0:1, :]
    reach = (2 * slots, ids.shape[1])
    row = iota(reach, 0)
    swap = jnp.where(odd == 0, slots, 0)
    place = jnp.where(row < slots, row + swap, row - swap) + nodes
    spread = (ids == place.astype(F32)).astype(F32).astype(BF16)
    for w in range(waves):
        for g in range(groups):
            for h in range(halves):
                owner = (w * groups + g) * halves + h
                gathered[g * rows : (g + 1) * rows, h * LANES : (h + 1) * LANES] = sums_ref[
                    owner, :rows, :
                ].astype(F32)
            inverses[g * patches : (g + 1) * patches, :] = sums_ref[
                (w * groups + g) * halves, rows : rows + patches, :
            ].astype(F32)
        grown = dot(grow, inverses[...].astype(BF16))
        folded = dot(jnp.where(in_lanes, grown, 0.0).astype(BF16), fold)
        inverse = jnp.where(in_patch, folded, 0.0).astype(BF16)
        coef = dot(inverse, gathered[...].astype(BF16)).astype(BF16)
        coef_ref[w] = coef
        if w == 0:
            for moved in arriving:
                moved.wait()
        for q in range(2):
            k = 2 * w + q
            margin = (dot(spread, other_ref[k]) + dot(brem_ref[k], coef)).astype(BF16)
            near_ref[k] = margin[:slots]
            far_ref[k] = margin[slots:]


def coefficients(odd, sums, b_ext, rest_ids, others, patches, slots, per_group):
    parts, _, columns = b_ext.shape
    width = others[0].shape[2]
    groups = columns // (patches * per_group)
    margin = ((parts, slots, width), BF16)
    return call(
        functools.partial(coef_kernel, per_group, patches),
        6,
        [odd],
        [b_ext] + others,
        [sums, rest_ids],
        [],
        [((parts // 2, columns, width), BF16), margin, margin],
        [
            vmem((columns, width), F32),
            vmem((groups * patches, LANES), F32),
            vmem((parts, 2 * slots, columns), BF16),
            vmem((parts, rest_ids.shape[1], width), BF16),
            pltpu.SemaphoreType.DMA((2 + len(others),)),
        ],
    )


def own_kernel(odd_ref, bext_hbm, *refs):
    *pairs, rows_ref, rest_ref, pos_ref, coef_ref, out_ref, back_ref, bown_ref, local_ref, other_ref, sems = refs
    half = len(pairs) // 2
    parts, nodes, _ = out_ref.shape
    patches, patch_nodes = pos_ref.shape
    core = nodes // patches
    arriving = []
    for k in range(parts):
        moves = [(bext_hbm.at[k, pl.ds(0, nodes)], bown_ref.at[k])]
        start = 0
        for a in pairs[half:]:
            moves.append((a.at[k], other_ref.at[k, pl.ds(start, a.shape[1])]))
            start += a.shape[1]
        start = 0
        terms = pl.ds((k % 2) * patch_nodes, patch_nodes)
        for a in pairs[:half]:
            here = pl.ds(start, a.shape[0])
            moves.append((a.at[:, k // 2, terms], local_ref.at[k, here]))
            start += a.shape[0]
        arriving.append([copy(m[0], m[1], sems.at[k, i], int(k > 1)) for i, m in enumerate(moves)])
    slots = rows_ref.shape[1]
    for b, ids in enumerate(partner_rows(rows_ref, odd_ref[0])):
        back_ref[:, b * slots : (b + 1) * slots] = (
            (ids == iota((nodes, slots), 0).astype(F32)).astype(F32).astype(BF16)
        )
    ids = rest_ref[0:1, :]
    shape = (nodes, ids.shape[1])
    spread = (ids == iota(shape, 0).astype(F32)).astype(F32).astype(BF16)
    places = iota((core, patch_nodes), 0).astype(F32)
    backs = [
        (pos_ref[p : p + 1, :] == places).astype(F32).astype(BF16) for p in range(patches)
    ]
    width = out_ref.shape[2]
    for k in range(0, parts, 2):
        for moved in arriving[k] + arriving[k + 1]:
            moved.wait()
        total = dot(spread, beside([other_ref[k], other_ref[k + 1]]))
        cores = [
            dot(backs[p], beside([local_ref[k, p], local_ref[k + 1, p]])) for p in range(patches)
        ]
        total = total + jnp.concatenate(cores, axis=0)
        for j in range(2):
            coarse = dot(bown_ref[k + j], coef_ref[(k + j) // 2])
            out_ref[k + j] = total[:, j * width : (j + 1) * width] + coarse


def own_rows(odd, b_ext, coef, rows, rest_ids, pos, locals_, others, nodes):
    parts, _, columns = b_ext.shape
    width = coef.shape[2]
    return call(
        own_kernel,
        20,
        [odd],
        [b_ext] + locals_ + others,
        [rows, rest_ids, pos, coef],
        [],
        [((parts, nodes, width), F32), ((nodes, 2 * rows.shape[1]), BF16)],
        [
            vmem((parts, nodes, columns), BF16),
            vmem((parts,) + pos.shape + (width,), BF16),
            vmem((parts, rest_ids.shape[1], width), BF16),
            pltpu.SemaphoreType.DMA((parts, 1 + len(locals_) + len(others))),
        ],
    )


def final_kernel(own_ref, spread_ref, near_ref, other_ref, out_hbm, out_ref, sems):
    parts, _, width = own_ref.shape
    sent = []
    for k in range(0, parts, 2):
        back = jnp.concatenate(
            [beside([a[k], a[k + 1]]) for a in (near_ref, other_ref)], axis=0
        )
        total = dot(spread_ref[...], back)
        for j in range(2):
            mine = total[:, j * width : (j + 1) * width]
            out_ref[k + j] = (own_ref[k + j] + mine).astype(BF16)
            sent.append(copy(out_ref.at[k + j], out_hbm.at[k + j], sems.at[k + j], j))
    for moved in sent:
        moved.wait()


def finish(own, spread, near, other):
    return call(
        final_kernel,
        12,
        [],
        [],
        [own, spread, near, other],
        [(own.shape, BF16)],
        [],
        [vmem(own.shape, BF16), pltpu.SemaphoreType.DMA((own.shape[0],))],
    )[0]


def per_device(residual, patch_inv, coarse_basis, coarse_inv, patch_slots, send_rows, coarse_block):
    waves, _, nodes, width = residual.shape
    patches = patch_inv.shape[0]
    size = coarse_basis.shape[3]
    slots = send_rows.shape[2]
    ext = nodes + 2 * slots
    owners = lax.axis_size(AXES)
    halves = width // LANES
    groups = owners // (waves * halves)
    per_group = size // groups
    assert owners % 2 == 0 and groups * waves * halves == owners and per_group * groups == size
    blocks = coarse_inv.shape[0]
    share = -(-blocks // lax.axis_size("patch"))
    rows = patches * per_group
    padded = -(-(rows + patches + share) // 8) * 8
    half = patches // 2
    send = send_rows[0]
    odd = (lax.axis_index(AXES) % 2).astype(jnp.int32).reshape(1)
    basis_t = jnp.swapaxes(coarse_basis, 2, 3)

    x_all = residual.reshape(2 * waves, nodes, width)
    to_first, to_second, slots_v = select_rows(x_all, send, patch_slots, odd)
    first_rows = swapped(to_first, AXES, False)
    second_rows = swapped(to_second, AXES, True)
    crem, y, b_ext, pos, rest_ids, r_own, bt_rem, lines = prepare(
        slots_v, basis_t, coarse_inv, x_all, ext, per_group, share
    )
    far, sent = restrict(
        coarse_block, odd, r_own, bt_rem, first_rows, second_rows, lines,
        owners, per_group, padded,
    )
    got = lax.all_to_all(sent, AXES, 0, 0, tiled=True)
    local_a, rest_a = local_products(pos, x_all, y, crem, far, patch_inv, 0, half)
    sums = owner_sums(got, patches, per_group, blocks, share)
    mine = lax.all_to_all(sums, AXES, 0, 0, tiled=True)
    local_b, rest_b = local_products(pos, x_all, y, crem, far, patch_inv, half, patches - half)
    coef, to_first, to_second = coefficients(
        odd, mine, b_ext, rest_ids, [rest_a, rest_b], patches, slots, per_group
    )
    first_back = swapped(to_first, AXES, False)
    second_back = swapped(to_second, AXES, True)
    own, spread = own_rows(odd, b_ext, coef, send, rest_ids, pos, [local_a, local_b], [rest_a, rest_b], nodes)
    out = finish(own, spread, first_back, second_back)
    return out.reshape(residual.shape)


def solution(mesh):
    placed = (
        P(None, None, AXES, None),
        P(AXES, None, None, None),
        P(AXES, None, None, None),
        P("coarse", None, None, None),
        P(AXES, None),
        P(AXES, None, None),
        P(AXES),
    )
    return jax.shard_map(
        per_device,
        mesh=mesh,
        in_specs=placed,
        out_specs=P(None, None, AXES, None),
        check_vma=False,
    )
```
